128 devices in a mesh: ctx: 32 (over x, z, core), head: 4 (over y).
Axes of the slice: x: 4, y: 4, z: 4, core: 2. Of those that a mesh axis runs over, the one named last changes fastest.
Arguments:
- queries: bfloat16 [32768, 4, 4, 128], P('ctx', None, 'head'), may hold values from -4.5 to 4.5
- key_rows: bfloat16 [32768, 4, 128], P('ctx'), may hold values from -3 to 3
- value_rows: bfloat16 [32768, 4, 128], P('ctx'), may hold values from -6 to 6
- out_grad: bfloat16 [32768, 4, 4, 128], P('ctx', None, 'head'), may hold values from -18 to 18
- outputs: bfloat16 [32768, 4, 4, 128], P('ctx', None, 'head'), may hold values from -6 to 6
- logsumexp: float32 [4, 4, 32768], P(None, 'head', 'ctx'), as said below
- selections: int32 [256, 3], P('ctx'), may hold values from 0 to 31, as said below
Outputs:
- grad_queries: bfloat16 [32768, 4, 4, 128], P('ctx', None, 'head')
- grad_keys: bfloat16 [32768, 4, 128], P('ctx', 'head')
- grad_values: bfloat16 [32768, 4, 128], P('ctx', 'head')
The draws below stay inside these ranges and needn't reach their ends.
Inputs may be any that keep to these rules, and one draw needn't show every extreme that they name: `selections`: column 0 of row b is the query block's own key block b // 8; columns 1 and 2 each name an earlier key block or repeat the own block, and two earlier blocks in one row differ. The query blocks of one key block never name the same earlier block twice. For every key block after the first, exactly one of its query blocks names key block 0. `logsumexp`: the log-sum-exp of scores over each query's attended keys, computed from queries and key_rows as in the reference program.
All inputs are finite; a program needn't handle non-finite values.
Results may differ from the reference program's by a relative error of at most 0.005.
Values may be sent and summed in bfloat16 or wider, within the bound.
No kernel may reach another device: no remote copies, remote signals or barrier semaphores. Data moves between devices by JAX's collectives and lax.ppermute only.
A program may use at most 128 MiB of HBM per device.

```python
import jax
import jax.numpy as jnp
from jax import lax

CTX_DEV = 1024
QB = 128
KV = 4
GROUP = 4
HD = 128
TOKENS = 32768
NQB = 256


def moba_rows(base_key, shape, bound):
    return jnp.clip(jax.random.normal(base_key, shape, jnp.float32), -3.0, 3.0) * (bound / 3.0)


def moba_queries(base_key):
    return moba_rows(jax.random.fold_in(base_key, 11), (TOKENS, KV, GROUP, HD), 4.5).astype(jnp.bfloat16)


def moba_keys(base_key):
    return moba_rows(jax.random.fold_in(base_key, 12), (TOKENS, KV, HD), 3.0).astype(jnp.bfloat16)


def moba_selections(base_key):
    table_key = jax.random.fold_in(base_key, 13)
    first_key, second_key = jax.random.split(table_key)
    block_count = TOKENS // CTX_DEV
    per_block = CTX_DEV // QB
    raw = jax.random.randint(first_key, (block_count, block_count), 0, 2 ** 20)
    columns = jnp.arange(block_count, dtype=jnp.int32)[None, :]
    rows_idx = jnp.arange(block_count, dtype=jnp.int32)[:, None]
    score = raw * block_count + columns
    score = jnp.where(columns == 0, -1, score)
    score = jnp.where(columns >= rows_idx, 2 ** 30, score)
    ordering = jnp.argsort(score, axis=1).astype(jnp.int32)
    offsets = jax.random.randint(second_key, (block_count,), 0, per_block)
    query_ids = jnp.arange(block_count * per_block, dtype=jnp.int32)
    owner = query_ids // per_block
    within = query_ids % per_block
    place = (within + offsets[owner]) % per_block

    def pick(position):
        safe = jnp.minimum(position, block_count - 1)
        return jnp.where(position < owner, ordering[owner, safe], owner)
    return jnp.stack([owner, pick(2 * place), pick(2 * place + 1)], axis=1).astype(jnp.int32)


def moba_logsumexp(base_key):
    queries = moba_queries(base_key).astype(jnp.float32)
    key_rows = moba_keys(base_key).astype(jnp.float32)
    chosen_all = moba_selections(base_key)
    scale = HD ** (-0.5)

    def one_block(block_idx):
        first = (block_idx * QB).astype(jnp.int32)
        q_blk = lax.dynamic_slice_in_dim(queries, first, QB, 0)
        chosen = chosen_all[block_idx]
        valid = jnp.stack([chosen[0] == chosen[0], chosen[1] != chosen[0], (chosen[2] != chosen[0]) & (chosen[2] != chosen[1])])
        starts = (chosen * CTX_DEV).astype(jnp.int32)
        key_sel = jnp.stack([lax.dynamic_slice_in_dim(key_rows, starts[j], CTX_DEV, 0) for j in range(3)])
        q_pos = first + jnp.arange(QB, dtype=jnp.int32)
        k_pos = starts[:, None] + jnp.arange(CTX_DEV, dtype=jnp.int32)[None, :]
        allowed = valid[None, :, None] & (k_pos[None, :, :] <= q_pos[:, None, None])
        scores = jnp.einsum('qkgd,jckd->kgqjc', q_blk, key_sel) * scale
        masked = jnp.where(allowed, scores, -1e+30)
        top = jnp.max(masked, axis=(3, 4), keepdims=True)
        total = jnp.sum(jnp.where(allowed, jnp.exp(masked - top), 0.0), axis=(3, 4))
        return top[:, :, :, 0, 0] + jnp.log(total)
    stacked = lax.map(one_block, jnp.arange(NQB, dtype=jnp.int32))
    return jnp.transpose(stacked, (1, 2, 0, 3)).reshape(KV, GROUP, TOKENS)


def draw_queries(key, part):
    return moba_queries(key)


def draw_key_rows(key, part):
    return moba_keys(key)


def draw_selections(key, part):
    return moba_selections(key)


def draw_logsumexp(key, part):
    return moba_logsumexp(key).astype(jnp.float32)


def block_levels(rng, shape, cuts, smallest, top_value):
    level = 1.0
    for dim, blocks in cuts:
        heights = jax.random.uniform(jax.random.fold_in(jax.random.fold_in(rng, 6), dim), (blocks,), jnp.float32, smallest / len(cuts), top_value / len(cuts))
        level = level * jnp.repeat(jnp.exp(heights), shape[dim] // blocks).reshape((-1,) + (1,) * (len(shape) - 1 - dim))
    return level


def noise(key, extent, width, most, cuts=(), held_as=jnp.bfloat16):
    array = width * jax.random.normal(key, extent, jnp.float32)
    if cuts:
        array = array * block_levels(key, extent, cuts, -0.22, 0.18)
    return jnp.clip(array, -most, most).astype(held_as)


def setup_inputs(seed: int = 0) -> dict:
    key_list = jax.random.split(jax.random.key(seed), 8)
    queries = draw_queries(jax.random.fold_in(key_list[7], 71), 0)
    key_rows = draw_key_rows(jax.random.fold_in(key_list[7], 71), 0)
    value_rows = noise(key_list[2], (TOKENS, KV, HD), 1.0, 6.0, ((0, 32),))
    out_grad = noise(key_list[3], (TOKENS, KV, GROUP, HD), 3.0, 18.0, ((0, 32), (2, 4)))
    outputs = noise(key_list[4], (TOKENS, KV, GROUP, HD), 1.0, 6.0, ((0, 32), (2, 4)))
    logsumexp = draw_logsumexp(jax.random.fold_in(key_list[7], 71), 0)
    selections = draw_selections(jax.random.fold_in(key_list[7], 71), 0)
    return {"queries": queries, "key_rows": key_rows, "value_rows": value_rows, "out_grad": out_grad, "outputs": outputs, "logsumexp": logsumexp, "selections": selections}


def reference(queries, key_rows, value_rows, out_grad, outputs, logsumexp, selections):
    token_count = queries.shape[0]
    scale = HD ** -0.5
    block_total = token_count // QB
    delta_all = jnp.sum(out_grad.astype(jnp.float32) * outputs.astype(jnp.float32), axis=-1)
    zero_rows = jnp.zeros(key_rows.shape, jnp.float32)

    def one_block(carry, block_idx):
        grad_k, grad_v = carry
        first = (block_idx * QB).astype(jnp.int32)
        q_blk = lax.dynamic_slice_in_dim(queries, first, QB, 0).astype(jnp.float32)
        g_blk = lax.dynamic_slice_in_dim(out_grad, first, QB, 0).astype(jnp.float32)
        lse_blk = lax.dynamic_slice_in_dim(logsumexp, first, QB, 2)
        delta_blk = jnp.transpose(lax.dynamic_slice_in_dim(delta_all, first, QB, 0), (1, 2, 0))
        chosen = selections[block_idx]
        valid = jnp.stack([chosen[0] == chosen[0], chosen[1] != chosen[0], (chosen[2] != chosen[0]) & (chosen[2] != chosen[1])])
        starts = (chosen * CTX_DEV).astype(jnp.int32)
        key_sel = jnp.stack([lax.dynamic_slice_in_dim(key_rows, starts[j], CTX_DEV, 0) for j in range(3)]).astype(jnp.float32)
        value_sel = jnp.stack([lax.dynamic_slice_in_dim(value_rows, starts[j], CTX_DEV, 0) for j in range(3)]).astype(jnp.float32)
        q_pos = first + jnp.arange(QB, dtype=jnp.int32)
        k_pos = starts[:, None] + jnp.arange(CTX_DEV, dtype=jnp.int32)[None, :]
        allowed = valid[None, :, None] & (k_pos[None, :, :] <= q_pos[:, None, None])
        scores = jnp.einsum('qkgd,jckd->kgqjc', q_blk, key_sel) * scale
        prob = jnp.where(allowed, jnp.exp(scores - lse_blk[..., None, None]), 0.0)
        dprob = jnp.einsum('qkgd,jckd->kgqjc', g_blk, value_sel)
        dscore = prob * (dprob - delta_blk[..., None, None])
        prob_low = lax.optimization_barrier(prob.astype(jnp.bfloat16)).astype(jnp.float32)
        dscore_low = lax.optimization_barrier(dscore.astype(jnp.bfloat16)).astype(jnp.float32)
        grad_q = jnp.einsum('kgqjc,jckd->qkgd', dscore_low, key_sel) * scale
        part_k = jnp.einsum('kgqjc,qkgd->jckd', dscore_low, q_blk) * scale
        part_v = jnp.einsum('kgqjc,qkgd->jckd', prob_low, g_blk)
        for j in range(3):
            old_k = lax.dynamic_slice_in_dim(grad_k, starts[j], CTX_DEV, 0)
            grad_k = lax.dynamic_update_slice_in_dim(grad_k, old_k + part_k[j], starts[j], 0)
            old_v = lax.dynamic_slice_in_dim(grad_v, starts[j], CTX_DEV, 0)
            grad_v = lax.dynamic_update_slice_in_dim(grad_v, old_v + part_v[j], starts[j], 0)
        return (grad_k, grad_v), grad_q.astype(jnp.bfloat16)

    (grad_k, grad_v), grad_q = lax.scan(one_block, (zero_rows, zero_rows), jnp.arange(block_total, dtype=jnp.int32))
    return grad_q.reshape(queries.shape), grad_k.astype(jnp.bfloat16), grad_v.astype(jnp.bfloat16)
```

```python
import functools
import math

import jax
import jax.numpy as jnp
from jax import lax
from jax.experimental import pallas as pl
from jax.experimental.pallas import tpu as pltpu
from jax.sharding import PartitionSpec as P


QB = 128
SIDE = 4
TILE = 256
OWN_TILE = 512
PIECES = 2
VMEM_LIMIT = 60 * 1024 * 1024
LOG2E = math.log2(math.e)


NT = (((1,), (1,)), ((), ()))
NN = (((1,), (0,)), ((), ()))
TN = (((0,), (0,)), ((), ()))


def dot(a, b, dims):
    return lax.dot_general(a, b, dims, preferred_element_type=jnp.float32)


def pairs(place):
    found = []
    for x in range(SIDE):
        for z in range(SIDE):
            for core in range(2):
                to_x, to_z, to_core = place(x, z, core)
                target = (to_x % SIDE * SIDE + to_z % SIDE) * 2 + to_core
                found.append(((x * SIDE + z) * 2 + core, target))
    return found


def shift(value, phase, step):
    def place(x, z, core):
        along_x = step if core == phase else 0
        return x + along_x, z + step - along_x, core

    return lax.ppermute(value, "ctx", pairs(place))


def other_core(value):
    return lax.ppermute(value, "ctx", pairs(lambda x, z, core: (x, z, 1 - core)))


def tile_grads(keys, values, q, g, lse, delta, scale2, mask=None):
    prob = jnp.exp2(dot(keys, q, NT) * scale2 - lse)
    if mask is not None:
        prob = jnp.where(mask, prob, 0.0)
    dscore = prob * (dot(values, g, NT) - delta)
    prob_low = prob.astype(jnp.bfloat16)
    dscore_low = dscore.astype(jnp.bfloat16)
    return dot(dscore_low, q, NN), dot(prob_low, g, NN), dot(dscore_low, keys, TN)


def own_kernel(scale2, q_ref, g_ref, st_ref, k_ref, v_ref, dq_ref, dk_ref, dv_ref):
    block = pl.program_id(0)

    @pl.when(block == 0)
    def _():
        dk_ref[...] = jnp.zeros_like(dk_ref)
        dv_ref[...] = jnp.zeros_like(dv_ref)

    rows = q_ref.shape[0] * QB
    q = q_ref[...].reshape(rows, -1)
    g = g_ref[...].reshape(rows, -1)
    lse = st_ref[0, 0:1, :]
    delta = st_ref[0, 1:2, :]
    ahead = lax.broadcasted_iota(jnp.int32, (OWN_TILE, rows), 0) - (
        lax.broadcasted_iota(jnp.int32, (OWN_TILE, rows), 1) & (QB - 1)
    )

    def step(tile, masked):
        where = pl.ds(tile * OWN_TILE, OWN_TILE)
        mask = ahead <= block * QB - tile * OWN_TILE if masked else None
        dk, dv, dq = tile_grads(
            k_ref[where, :], v_ref[where, :], q, g, lse, delta, scale2, mask
        )
        dk_ref[where, :] += dk
        dv_ref[where, :] += dv
        return dq

    reach = OWN_TILE // QB
    for last in range(k_ref.shape[0] // OWN_TILE):

        @pl.when(block // reach == last)
        def _():
            dq = step(last, True)
            for tile in range(last):
                dq += step(tile, False)
            dq_ref[...] = dq.reshape(dq_ref.shape)


def own_grads(packed, stats, keys, values, scale2):
    heads, _, width = packed.shape
    rows = keys.shape[0]
    blocks = rows // QB
    q_spec = pl.BlockSpec((heads, QB, width), lambda b: (0, b, 0))
    g_spec = pl.BlockSpec((heads, QB, width), lambda b: (0, b + blocks, 0))
    whole = pl.BlockSpec((rows, width), lambda b: (0, 0))
    acc = jax.ShapeDtypeStruct(keys.shape, jnp.float32)
    return pl.pallas_call(
        functools.partial(own_kernel, scale2),
        grid=(blocks,),
        in_specs=[q_spec, g_spec, pl.BlockSpec((1, 2, heads * QB), lambda b: (b, 0, 0)), whole, whole],
        out_specs=[q_spec, whole, whole],
        out_shape=[jax.ShapeDtypeStruct((heads, rows, width), jnp.float32), acc, acc],
        compiler_params=pltpu.CompilerParams(vmem_limit_bytes=VMEM_LIMIT),
        cost_estimate=pl.CostEstimate(
            flops=6 * heads * rows * rows * width, bytes_accessed=8 << 20, transcendentals=0
        ),
        name="own",
    )(packed, packed, stats, keys, values)


def remote_kernel(scale2, bases, fresh, tbl, *refs):
    sources = len(bases) * PIECES
    q0, g0, q1, g1, st0, st1, in0 = refs[:7]
    rest = refs[7:]
    if not fresh:
        in1, rest = rest[0], rest[1:]
    blocks = rest[:sources]
    dq0, dq1 = rest[sources : sources + 2]
    outs = rest[sources + 2 : -1]
    buf = rest[-1]
    at = pl.program_id(0)
    heads = q0.shape[0]
    rows = heads * QB
    span = SIDE // PIECES

    @pl.when(at == 0)
    def _():
        dq0[...] = in0[...]
        dq1[...] = jnp.zeros_like(dq1) if fresh else in1[...]

    for i, block_ref in enumerate(blocks):

        @pl.when(at // span == i)
        def _():
            buf[...] = block_ref[0]

    entry = at % SIDE + bases[0]
    for i in range(1, len(bases)):
        entry = jnp.where(at // SIDE == i, at % SIDE + bases[i], entry)
    own = tbl[entry]
    sib = tbl[SIDE * SIDE + entry]

    def load(block, q_ref, g_ref, st_ref):
        where = pl.ds(pl.multiple_of(block * QB, QB), QB)
        stats = st_ref[block]
        return (
            q_ref[:, where, :].reshape(rows, -1),
            g_ref[:, where, :].reshape(rows, -1),
            stats[0:1, :],
            stats[1:2, :],
        )

    def run(sides):
        loaded = [load(block, *side[:3]) for block, side in sides]
        total = [None] * len(sides)
        for tile in range(buf.shape[1] // TILE):
            where = pl.ds(tile * TILE, TILE)
            keys, values = buf[0, where, :], buf[1, where, :]
            dk_sum, dv_sum = None, None
            for i, (q, g, lse, delta) in enumerate(loaded):
                dk, dv, dq = tile_grads(keys, values, q, g, lse, delta, scale2)
                dk_sum = dk if dk_sum is None else dk_sum + dk
                dv_sum = dv if dv_sum is None else dv_sum + dv
                total[i] = dq if total[i] is None else total[i] + dq
            buf[0, where, :] = dk_sum.astype(jnp.bfloat16)
            buf[1, where, :] = dv_sum.astype(jnp.bfloat16)
        for (block, side), dq in zip(sides, total):
            where = pl.ds(pl.multiple_of(block * QB, QB), QB)
            side[3][:, where, :] += dq.reshape(heads, QB, -1)

    own_side = (own, (q0, g0, st0, dq0))
    sib_side = (sib, (q1, g1, st1, dq1))

    @pl.when((own >= 0) & (sib >= 0))
    def _():
        run([own_side, sib_side])

    @pl.when((own >= 0) & (sib < 0))
    def _():
        run([own_side])

    @pl.when((own < 0) & (sib >= 0))
    def _():
        run([sib_side])

    @pl.when((own < 0) & (sib < 0))
    def _():
        buf[...] = jnp.zeros_like(buf)

    for i, out_ref in enumerate(outs):

        @pl.when(at // SIDE == i)
        def _():
            out_ref[0] = buf[...]


def remote_grads(table, own, sib, stats, sources, bases, carried, scale2):
    heads, _, width = own.shape
    rows = stats[0].shape[0] * QB
    count = len(bases)
    span = SIDE // PIECES
    once = pl.Buffered(1)
    q_spec = pl.BlockSpec((heads, rows, width), lambda k, t: (0, 0, 0), pipeline_mode=once)
    g_spec = pl.BlockSpec((heads, rows, width), lambda k, t: (0, 1, 0), pipeline_mode=once)
    stat = pl.BlockSpec(stats[0].shape, lambda k, t: (0, 0, 0))
    acc_spec = pl.BlockSpec((heads, rows, width), lambda k, t: (0, 0, 0))

    def piece(size, i):
        return pl.BlockSpec(
            (1, 2, rows, width), lambda k, t: (jnp.clip(k - size * i, 0, size - 1), 0, 0, 0)
        )

    operands = [array for source in sources for array in source]
    acc = jax.ShapeDtypeStruct((heads, rows, width), jnp.float32)
    part = jax.ShapeDtypeStruct((SIDE, 2, rows, width), jnp.bfloat16)
    return pl.pallas_call(
        functools.partial(remote_kernel, scale2, bases, len(carried) == 1),
        grid_spec=pltpu.PrefetchScalarGridSpec(
            num_scalar_prefetch=1,
            grid=(SIDE * count,),
            in_specs=[q_spec, g_spec, q_spec, g_spec, stat, stat]
            + [q_spec] * len(carried)
            + [piece(span, i) for i in range(len(operands))],
            out_specs=[acc_spec, acc_spec] + [piece(SIDE, i) for i in range(count)],
            scratch_shapes=[pltpu.VMEM((2, rows, width), jnp.bfloat16)],
        ),
        out_shape=[acc, acc] + [part] * count,
        compiler_params=pltpu.CompilerParams(vmem_limit_bytes=VMEM_LIMIT),
        cost_estimate=pl.CostEstimate(
            flops=SIDE * count * 10 * heads * QB * rows * width,
            bytes_accessed=(12 + 4 * count) << 20,
            transcendentals=0,
        ),
        name="remote",
    )(table, own, own, sib, sib, *stats, *carried, *operands)


def split3(value):
    terms = []
    for _ in range(3):
        term = lax.reduce_precision(value, 8, 7)
        terms.append(term.astype(jnp.bfloat16))
        value = value - term
    return jnp.stack(terms, axis=-2)


def grads(queries, key_rows, value_rows, out_grad, outputs, logsumexp, selections):
    rows, kv_heads, _, width = queries.shape
    blocks = rows // QB
    scale = width ** (-0.5)
    scale2 = scale * LOG2E
    me = lax.axis_index("ctx")
    head = lax.axis_index("head")
    x, z, core = me // (2 * SIDE), (me // 2) % SIDE, me % 2

    keys = lax.dynamic_index_in_dim(key_rows, head, 1, keepdims=False)
    values = lax.dynamic_index_in_dim(value_rows, head, 1, keepdims=False)
    both = jnp.stack([keys, values])
    behind = shift(both, 0, 1)
    ahead = shift(both, 0, -1)
    across = shift(both, 0, 2)
    first = jnp.stack([both, behind])
    second = jnp.stack([across, ahead])
    line = (first, second)
    line_behind = (shift(first, 1, 1), shift(second, 1, 1))
    line_ahead = (shift(first, 1, -1), shift(second, 1, -1))
    line_across = (shift(line_behind[0], 1, 1), shift(line_ahead[1], 1, -1))

    def turn(value):
        return lax.all_to_all(value, "head", split_axis=0, concat_axis=0, tiled=True)

    delta = jnp.sum(out_grad.astype(jnp.float32) * outputs.astype(jnp.float32), axis=-1)
    stats = jnp.stack([logsumexp[:, 0] * LOG2E, delta[:, :, 0].T], axis=1)
    stats = split3(stats.reshape(kv_heads, 2, rows)).reshape(kv_heads, -1, width)
    own = turn(
        jnp.concatenate(
            [
                jnp.transpose(queries[:, :, 0], (1, 0, 2)),
                jnp.transpose(out_grad[:, :, 0], (1, 0, 2)),
                stats,
            ],
            axis=1,
        ),
    )
    sib = other_core(own)
    sib_selections = other_core(selections)

    def stats_of(packed):
        terms = packed[:, 2 * rows :].reshape(-1, 2, 3, blocks, QB).astype(jnp.float32)
        return (terms[:, :, 0] + terms[:, :, 1] + terms[:, :, 2]).transpose(2, 1, 0, 3).reshape(blocks, 2, -1)

    own_stats, sib_stats = stats_of(own), stats_of(sib)

    index = jnp.arange(SIDE * SIDE, dtype=jnp.int32)
    near, far = index % SIDE, index // SIDE
    back_x, back_z = jnp.where(core == 0, near, far), jnp.where(core == 0, far, near)
    source = (((x - back_x) % SIDE) * SIDE + (z - back_z) % SIDE) * 2 + core

    def listed(picks, device):
        hit = ((picks[:, 1:2] == source) | (picks[:, 2:3] == source)) & (source != device)
        return jnp.max(jnp.where(hit, jnp.arange(blocks, dtype=jnp.int32)[:, None], -1), axis=0)

    table = jnp.concatenate([listed(selections, me), listed(sib_selections, me + 1 - 2 * core)])

    def remote(sources, bases, carried):
        return remote_grads(
            table, own, sib, (own_stats, sib_stats), sources, bases, carried, scale2
        )

    own_q, own_k, own_v = own_grads(own, own_stats, keys, values, scale2)
    dq0, dq1, part_behind, part_ahead = remote(
        [line_behind, line_ahead], (SIDE, 3 * SIDE), (own_q,)
    )
    back_behind = shift(part_behind, 1, -1)
    back_ahead = shift(part_ahead, 1, 1)
    dq0, dq1, part_across, part_line = remote(
        [line_across, line], (2 * SIDE, 0), (dq0, dq1)
    )
    back_across = shift(part_across, 1, 2)

    total = [
        sum(part[i].astype(jnp.float32) for part in (part_line, back_behind, back_ahead, back_across))
        for i in range(SIDE)
    ]
    low = [part.astype(jnp.bfloat16) for part in total[1:]]
    near_sum = (
        total[0]
        + shift(low[0], 0, -1).astype(jnp.float32)
        + shift(low[2], 0, 1).astype(jnp.float32)
        + shift(low[1], 0, 2).astype(jnp.float32)
    )
    grad_k = ((near_sum[0] + own_k) * scale).astype(jnp.bfloat16)
    grad_v = (near_sum[1] + own_v).astype(jnp.bfloat16)

    dq_low = dq1.astype(jnp.bfloat16)
    returned = other_core(dq_low)
    dq = ((dq0 + returned.astype(jnp.float32)) * scale).astype(jnp.bfloat16)
    dq = jnp.transpose(turn(dq), (1, 0, 2))[:, :, None]
    return dq, grad_k[:, None], grad_v[:, None]


def solution(mesh):
    in_specs = (
        P("ctx", None, "head", None),
        P("ctx", None, None),
        P("ctx", None, None),
        P("ctx", None, "head", None),
        P("ctx", None, "head", None),
        P(None, "head", "ctx"),
        P("ctx", None),
    )
    out_specs = (P("ctx", None, "head", None), P("ctx", "head", None), P("ctx", "head", None))
    return jax.shard_map(grads, mesh=mesh, in_specs=in_specs, out_specs=out_specs, check_vma=False)
```

```python
import functools
import math

import jax
import jax.numpy as jnp
from jax import lax
from jax.experimental import pallas as pl
from jax.experimental.pallas import tpu as pltpu
from jax.sharding import PartitionSpec as P


QB = 128
SIDE = 4
TILE = 256
UNROLL = 2
OWN_TILE = 512
VMEM_LIMIT = 60 * 1024 * 1024
LOG2E = math.log2(math.e)


NT = (((1,), (1,)), ((), ()))
NN = (((1,), (0,)), ((), ()))
TN = (((0,), (0,)), ((), ()))


def dot(a, b, dims):
    return lax.dot_general(a, b, dims, preferred_element_type=jnp.float32)


def pairs(place):
    found = []
    for x in range(SIDE):
        for z in range(SIDE):
            for core in range(2):
                to_x, to_z, to_core = place(x, z, core)
                target = (to_x % SIDE * SIDE + to_z % SIDE) * 2 + to_core
                found.append(((x * SIDE + z) * 2 + core, target))
    return found


def shift(value, phase, step):
    def place(x, z, core):
        along_x = step if core == phase else 0
        return x + along_x, z + step - along_x, core

    return lax.ppermute(value, "ctx", pairs(place))


def other_core(value):
    return lax.ppermute(value, "ctx", pairs(lambda x, z, core: (x, z, 1 - core)))


def tile_grads(keys, values, q, g, lse, delta, scale2, mask=None):
    prob = jnp.exp2(dot(keys, q, NT) * scale2 - lse)
    if mask is not None:
        prob = jnp.where(mask, prob, 0.0)
    dscore = prob * (dot(values, g, NT) - delta)
    prob_low = prob.astype(jnp.bfloat16)
    dscore_low = dscore.astype(jnp.bfloat16)
    return dot(dscore_low, q, NN), dot(prob_low, g, NN), dot(dscore_low, keys, TN)


def own_kernel(scale2, q_ref, g_ref, st_ref, k_ref, v_ref, dq_ref, dk_ref, dv_ref):
    block = pl.program_id(0)

    @pl.when(block == 0)
    def _():
        dk_ref[...] = jnp.zeros_like(dk_ref)
        dv_ref[...] = jnp.zeros_like(dv_ref)

    rows = q_ref.shape[0] * QB
    q = q_ref[...].reshape(rows, -1)
    g = g_ref[...].reshape(rows, -1)
    lse = st_ref[0, 0:1, :]
    delta = st_ref[0, 1:2, :]
    ahead = lax.broadcasted_iota(jnp.int32, (OWN_TILE, rows), 0) - (
        lax.broadcasted_iota(jnp.int32, (OWN_TILE, rows), 1) & (QB - 1)
    )

    def step(tile, masked):
        where = pl.ds(tile * OWN_TILE, OWN_TILE)
        mask = ahead <= block * QB - tile * OWN_TILE if masked else None
        dk, dv, dq = tile_grads(
            k_ref[where, :], v_ref[where, :], q, g, lse, delta, scale2, mask
        )
        dk_ref[where, :] += dk
        dv_ref[where, :] += dv
        return dq

    reach = OWN_TILE // QB
    for last in range(k_ref.shape[0] // OWN_TILE):

        @pl.when(block // reach == last)
        def _():
            dq = step(last, True)
            for tile in range(last):
                dq += step(tile, False)
            dq_ref[...] = dq.reshape(dq_ref.shape)


def own_grads(packed, stats, keys, values, scale2):
    heads, _, width = packed.shape
    rows = keys.shape[0]
    blocks = rows // QB
    q_spec = pl.BlockSpec((heads, QB, width), lambda b: (0, b, 0))
    g_spec = pl.BlockSpec((heads, QB, width), lambda b: (0, b + blocks, 0))
    whole = pl.BlockSpec((rows, width), lambda b: (0, 0))
    acc = jax.ShapeDtypeStruct(keys.shape, jnp.float32)
    return pl.pallas_call(
        functools.partial(own_kernel, scale2),
        grid=(blocks,),
        in_specs=[q_spec, g_spec, pl.BlockSpec((1, 2, heads * QB), lambda b: (b, 0, 0)), whole, whole],
        out_specs=[q_spec, whole, whole],
        out_shape=[jax.ShapeDtypeStruct((heads, rows, width), jnp.float32), acc, acc],
        compiler_params=pltpu.CompilerParams(vmem_limit_bytes=VMEM_LIMIT),
        cost_estimate=pl.CostEstimate(
            flops=6 * heads * rows * rows * width, bytes_accessed=8 << 20, transcendentals=0
        ),
        name="own",
    )(packed, packed, stats, keys, values)


def remote_kernel(scale2, bases, offsets, tbl, *refs):
    sources = len(offsets) - 1
    q0, g0, q1, g1, st0, st1 = refs[:6]
    blocks = refs[6 : 6 + sources]
    out0, out1 = refs[6 + sources : 8 + sources]
    outs = refs[8 + sources : -3]
    buf, dq0, dq1 = refs[-3:]
    at = pl.program_id(0)
    heads = q0.shape[0]
    rows = heads * QB

    @pl.when(at == 0)
    def _():
        dq0[...] = jnp.zeros_like(dq0)
        dq1[...] = jnp.zeros_like(dq1)

    for i, block_ref in enumerate(blocks):

        @pl.when((at >= offsets[i]) & (at < offsets[i + 1]))
        def _():
            buf[...] = block_ref[0]

    entry = at % SIDE + bases[0]
    for i in range(1, len(bases)):
        entry = jnp.where(at // SIDE == i, at % SIDE + bases[i], entry)
    own = tbl[entry]
    sib = tbl[SIDE * SIDE + entry]

    def load(block, q_ref, g_ref, st_ref):
        where = pl.ds(pl.multiple_of(block * QB, QB), QB)
        stats = st_ref[block]
        return (
            q_ref[:, where, :].reshape(rows, -1),
            g_ref[:, where, :].reshape(rows, -1),
            stats[0:1, :],
            stats[1:2, :],
        )

    def run(sides):
        loaded = [load(block, *side[:3]) for block, side in sides]

        @pl.loop(0, buf.shape[1] // (UNROLL * TILE))
        def _(turn):
            total = [None] * len(sides)
            for tile in range(UNROLL):
                where = pl.ds(pl.multiple_of((turn * UNROLL + tile) * TILE, TILE), TILE)
                keys, values = buf[0, where, :], buf[1, where, :]
                dk_sum, dv_sum = None, None
                for i, (q, g, lse, delta) in enumerate(loaded):
                    dk, dv, dq = tile_grads(keys, values, q, g, lse, delta, scale2)
                    dk_sum = dk if dk_sum is None else dk_sum + dk
                    dv_sum = dv if dv_sum is None else dv_sum + dv
                    total[i] = dq if total[i] is None else total[i] + dq
                buf[0, where, :] = dk_sum.astype(jnp.bfloat16)
                buf[1, where, :] = dv_sum.astype(jnp.bfloat16)
            for (block, side), dq in zip(sides, total):
                where = pl.ds(pl.multiple_of(block * QB, QB), QB)
                side[3][:, where, :] += dq.reshape(heads, QB, -1)

    own_side = (own, (q0, g0, st0, dq0))
    sib_side = (sib, (q1, g1, st1, dq1))

    @pl.when((own >= 0) & (sib >= 0))
    def _():
        run([own_side, sib_side])

    @pl.when((own >= 0) & (sib < 0))
    def _():
        run([own_side])

    @pl.when((own < 0) & (sib >= 0))
    def _():
        run([sib_side])

    @pl.when((own < 0) & (sib < 0))
    def _():
        buf[...] = jnp.zeros_like(buf)

    for i, out_ref in enumerate(outs):

        @pl.when(at // SIDE == i)
        def _():
            out_ref[0] = buf[...]

    @pl.when(at == pl.num_programs(0) - 1)
    def _():
        out0[...] = dq0[...].astype(out0.dtype)
        out1[...] = dq1[...].astype(out1.dtype)


def remote_grads(table, own, sib, stats, groups, bases, scale2):
    heads, _, width = own.shape
    rows = stats[0].shape[0] * QB
    count = len(bases)
    once = pl.Buffered(1)
    q_spec = pl.BlockSpec((heads, rows, width), lambda k, t: (0, 0, 0), pipeline_mode=once)
    g_spec = pl.BlockSpec((heads, rows, width), lambda k, t: (0, 1, 0), pipeline_mode=once)
    stat = pl.BlockSpec(stats[0].shape, lambda k, t: (0, 0, 0))
    acc_spec = pl.BlockSpec((heads, rows, width), lambda k, t: (0, 0, 0))

    def piece(start, size):
        return pl.BlockSpec(
            (1, 2, rows, width), lambda k, t: (jnp.clip(k - start, 0, size - 1), 0, 0, 0)
        )

    operands = [array for group in groups for array in group]
    offsets = [0]
    for array in operands:
        offsets.append(offsets[-1] + array.shape[0])
    acc = jax.ShapeDtypeStruct((heads, rows, width), jnp.bfloat16)
    part = jax.ShapeDtypeStruct((SIDE, 2, rows, width), jnp.bfloat16)
    return pl.pallas_call(
        functools.partial(remote_kernel, scale2, bases, offsets),
        grid_spec=pltpu.PrefetchScalarGridSpec(
            num_scalar_prefetch=1,
            grid=(SIDE * count,),
            in_specs=[q_spec, g_spec, q_spec, g_spec, stat, stat]
            + [piece(start, array.shape[0]) for start, array in zip(offsets, operands)],
            out_specs=[acc_spec, acc_spec] + [piece(SIDE * i, SIDE) for i in range(count)],
            scratch_shapes=[
                pltpu.VMEM((2, rows, width), jnp.bfloat16),
                pltpu.VMEM((heads, rows, width), jnp.float32),
                pltpu.VMEM((heads, rows, width), jnp.float32),
            ],
        ),
        out_shape=[acc, acc] + [part] * count,
        compiler_params=pltpu.CompilerParams(vmem_limit_bytes=VMEM_LIMIT),
        cost_estimate=pl.CostEstimate(
            flops=SIDE * count * 10 * heads * QB * rows * width,
            bytes_accessed=(8 + 4 * count) << 20,
            transcendentals=0,
        ),
        name="remote",
    )(table, own, own, sib, sib, *stats, *operands)


def split3(value):
    terms = []
    for _ in range(3):
        term = lax.reduce_precision(value, 8, 7)
        terms.append(term.astype(jnp.bfloat16))
        value = value - term
    return jnp.stack(terms, axis=-2)


def grads(queries, key_rows, value_rows, out_grad, outputs, logsumexp, selections):
    rows, kv_heads, _, width = queries.shape
    blocks = rows // QB
    scale = width ** (-0.5)
    scale2 = scale * LOG2E
    me = lax.axis_index("ctx")
    head = lax.axis_index("head")
    x, z, core = me // (2 * SIDE), (me // 2) % SIDE, me % 2

    keys = lax.dynamic_index_in_dim(key_rows, head, 1, keepdims=False)
    values = lax.dynamic_index_in_dim(value_rows, head, 1, keepdims=False)
    both = jnp.stack([keys, values])
    behind = shift(both, 0, 1)
    ahead = shift(both, 0, -1)
    across = shift(both, 0, 2)
    sides = jnp.stack([behind, ahead])
    line = (both[None], sides, across[None])
    line_behind = tuple(shift(piece, 1, 1) for piece in line)
    line_ahead = tuple(shift(piece, 1, -1) for piece in line)
    line_across = (
        shift(line_behind[0], 1, 1), shift(line_ahead[1], 1, -1), shift(line_behind[2], 1, 1)
    )

    def turn(value):
        return lax.all_to_all(value, "head", split_axis=0, concat_axis=0, tiled=True)

    delta = jnp.sum(out_grad.astype(jnp.float32) * outputs.astype(jnp.float32), axis=-1)
    stats = jnp.stack([logsumexp[:, 0] * LOG2E, delta[:, :, 0].T], axis=1)
    stats = split3(stats.reshape(kv_heads, 2, rows)).reshape(kv_heads, -1, width)
    own = turn(
        jnp.concatenate(
            [
                jnp.transpose(queries[:, :, 0], (1, 0, 2)),
                jnp.transpose(out_grad[:, :, 0], (1, 0, 2)),
                stats,
            ],
            axis=1,
        ),
    )
    sib = other_core(own)
    sib_selections = other_core(selections)

    def stats_of(packed):
        terms = packed[:, 2 * rows :].reshape(-1, 2, 3, blocks, QB).astype(jnp.float32)
        return (terms[:, :, 0] + terms[:, :, 1] + terms[:, :, 2]).transpose(2, 1, 0, 3).reshape(blocks, 2, -1)

    own_stats, sib_stats = stats_of(own), stats_of(sib)

    index = jnp.arange(SIDE * SIDE, dtype=jnp.int32)
    near, far = index % SIDE, index // SIDE
    near = jnp.where(near >= 2, 5 - near, near)
    back_x, back_z = jnp.where(core == 0, near, far), jnp.where(core == 0, far, near)
    source = (((x - back_x) % SIDE) * SIDE + (z - back_z) % SIDE) * 2 + core

    def listed(picks, device):
        hit = ((picks[:, 1:2] == source) | (picks[:, 2:3] == source)) & (source != device)
        return jnp.max(jnp.where(hit, jnp.arange(blocks, dtype=jnp.int32)[:, None], -1), axis=0)

    table = jnp.concatenate([listed(selections, me), listed(sib_selections, me + 1 - 2 * core)])

    def remote(groups, bases):
        return remote_grads(table, own, sib, (own_stats, sib_stats), groups, bases, scale2)

    level0, level1, part_line = remote([line], (0,))
    first0, first1, part_behind, part_ahead = remote([line_behind, line_ahead], (SIDE, 3 * SIDE))
    back_behind = shift(part_behind, 1, -1)
    back_ahead = shift(part_ahead, 1, 1)
    second0, second1, part_across = remote([line_across], (2 * SIDE,))
    back_across = shift(part_across, 1, 2)
    own_q, own_k, own_v = own_grads(own, own_stats, keys, values, scale2)

    def summed(*parts):
        return sum(part.astype(jnp.float32) for part in parts)

    total = [
        summed(part_line[i], back_behind[i], back_ahead[i], back_across[i])
        for i in range(SIDE)
    ]
    low = [part.astype(jnp.bfloat16) for part in total[1:]]
    near_sum = (
        total[0]
        + shift(low[0], 0, -1).astype(jnp.float32)
        + shift(low[1], 0, 1).astype(jnp.float32)
        + shift(low[2], 0, 2).astype(jnp.float32)
    )
    grad_k = ((near_sum[0] + own_k) * scale).astype(jnp.bfloat16)
    grad_v = (near_sum[1] + own_v).astype(jnp.bfloat16)

    dq_low = summed(level1, first1, second1).astype(jnp.bfloat16)
    returned = other_core(dq_low)
    dq = ((own_q + summed(level0, first0, second0, returned)) * scale).astype(jnp.bfloat16)
    dq = jnp.transpose(turn(dq), (1, 0, 2))[:, :, None]
    return dq, grad_k[:, None], grad_v[:, None]


def solution(mesh):
    in_specs = (
        P("ctx", None, "head", None),
        P("ctx", None, None),
        P("ctx", None, None),
        P("ctx", None, "head", None),
        P("ctx", None, "head", None),
        P(None, "head", "ctx"),
        P("ctx", None),
    )
    out_specs = (P("ctx", None, "head", None), P("ctx", "head", None), P("ctx", "head", None))
    return jax.shard_map(grads, mesh=mesh, in_specs=in_specs, out_specs=out_specs, check_vma=False)
```

```python
import functools
import math

import jax
import jax.numpy as jnp
from jax import lax
from jax.experimental import pallas as pl
from jax.experimental.pallas import tpu as pltpu
from jax.sharding import PartitionSpec as P


QB = 128
SIDE = 4
OWN_TILE = 512
VMEM_LIMIT = 60 * 1024 * 1024
LOG2E = math.log2(math.e)


NT = (((1,), (1,)), ((), ()))
NN = (((1,), (0,)), ((), ()))
TN = (((0,), (0,)), ((), ()))


def dot(a, b, dims):
    return lax.dot_general(a, b, dims, preferred_element_type=jnp.float32)


def pairs(place):
    found = []
    for x in range(SIDE):
        for z in range(SIDE):
            for core in range(2):
                to_x, to_z, to_core = place(x, z, core)
                target = (to_x % SIDE * SIDE + to_z % SIDE) * 2 + to_core
                found.append(((x * SIDE + z) * 2 + core, target))
    return found


def shift(value, phase, step):
    def place(x, z, core):
        along_x = step if core == phase else 0
        return x + along_x, z + step - along_x, core

    return lax.ppermute(value, "ctx", pairs(place))


def other_core(value):
    return lax.ppermute(value, "ctx", pairs(lambda x, z, core: (x, z, 1 - core)))


def tile_grads(keys, values, q, g, lse, delta, scale2, mask=None):
    prob = jnp.exp2(dot(keys, q, NT) * scale2 - lse)
    if mask is not None:
        prob = jnp.where(mask, prob, 0.0)
    dscore = prob * (dot(values, g, NT) - delta)
    prob_low = prob.astype(jnp.bfloat16)
    dscore_low = dscore.astype(jnp.bfloat16)
    return dot(dscore_low, q, NN), dot(prob_low, g, NN), dot(dscore_low, keys, TN)


def own_kernel(scale2, q_ref, g_ref, st_ref, k_ref, v_ref, dq_ref, dk_ref, dv_ref):
    block = pl.program_id(0)

    @pl.when(block == 0)
    def _():
        dk_ref[...] = jnp.zeros_like(dk_ref)
        dv_ref[...] = jnp.zeros_like(dv_ref)

    rows = q_ref.shape[0] * QB
    q = q_ref[...].reshape(rows, -1)
    g = g_ref[...].reshape(rows, -1)
    lse = st_ref[0, 0:1, :]
    delta = st_ref[0, 1:2, :]
    ahead = lax.broadcasted_iota(jnp.int32, (OWN_TILE, rows), 0) - (
        lax.broadcasted_iota(jnp.int32, (OWN_TILE, rows), 1) & (QB - 1)
    )

    def step(tile, masked):
        where = pl.ds(tile * OWN_TILE, OWN_TILE)
        mask = ahead <= block * QB - tile * OWN_TILE if masked else None
        dk, dv, dq = tile_grads(
            k_ref[where, :], v_ref[where, :], q, g, lse, delta, scale2, mask
        )
        dk_ref[where, :] += dk
        dv_ref[where, :] += dv
        return dq

    reach = OWN_TILE // QB
    for last in range(k_ref.shape[0] // OWN_TILE):

        @pl.when(block // reach == last)
        def _():
            dq = step(last, True)
            for tile in range(last):
                dq += step(tile, False)
            dq_ref[...] = dq.reshape(dq_ref.shape)


def own_grads(packed, stats, keys, values, scale2):
    heads, _, width = packed.shape
    rows = keys.shape[0]
    blocks = rows // QB
    q_spec = pl.BlockSpec((heads, QB, width), lambda b: (0, b, 0))
    g_spec = pl.BlockSpec((heads, QB, width), lambda b: (0, b + blocks, 0))
    whole = pl.BlockSpec((rows, width), lambda b: (0, 0))
    acc = jax.ShapeDtypeStruct(keys.shape, jnp.float32)
    return pl.pallas_call(
        functools.partial(own_kernel, scale2),
        grid=(blocks,),
        in_specs=[q_spec, g_spec, pl.BlockSpec((1, 2, heads * QB), lambda b: (b, 0, 0)), whole, whole],
        out_specs=[q_spec, whole, whole],
        out_shape=[jax.ShapeDtypeStruct((heads, rows, width), jnp.float32), acc, acc],
        compiler_params=pltpu.CompilerParams(vmem_limit_bytes=VMEM_LIMIT),
        cost_estimate=pl.CostEstimate(
            flops=6 * heads * rows * rows * width, bytes_accessed=8 << 20, transcendentals=0
        ),
        name="own",
    )(packed, packed, stats, keys, values)


def remote_kernel(scale2, bases, offsets, tbl, *refs):
    sources = len(offsets) - 1
    q0, g0, q1, g1, st0, st1 = refs[:6]
    blocks = refs[6 : 6 + sources]
    out0, out1 = refs[6 + sources : 8 + sources]
    outs = refs[8 + sources : -4]
    buf, q_buf, g_buf, dq = refs[-4:]
    at = pl.program_id(0)
    heads = q0.shape[0]
    rows = heads * QB

    @pl.when(at == 0)
    def _():
        dq[...] = jnp.zeros_like(dq)

    for i, block_ref in enumerate(blocks):

        @pl.when((at >= offsets[i]) & (at < offsets[i + 1]))
        def _():
            buf[...] = block_ref[0]

    entry = at % SIDE + bases[0]
    for i in range(1, len(bases)):
        entry = jnp.where(at // SIDE == i, at % SIDE + bases[i], entry)
    own = tbl[entry]
    sib = tbl[SIDE * SIDE + entry]

    def rows_of(block):
        return pl.ds(pl.multiple_of(block * QB, QB), QB)

    def load(block, q_ref, g_ref):
        where = rows_of(block)
        return q_ref[:, where, :].reshape(rows, -1), g_ref[:, where, :].reshape(rows, -1)

    def run(units):
        dk_sum, dv_sum = None, None
        for side, block, q, g, stats in units:
            dk, dv, dq_part = tile_grads(
                buf[0], buf[1], q, g, stats[0:1, :], stats[1:2, :], scale2
            )
            dk_sum = dk if dk_sum is None else dk_sum + dk
            dv_sum = dv if dv_sum is None else dv_sum + dv
            dq[side, :, rows_of(block), :] += dq_part.reshape(heads, QB, -1)
        buf[0] = dk_sum.astype(jnp.bfloat16)
        buf[1] = dv_sum.astype(jnp.bfloat16)

    @pl.when((own >= 0) & (sib >= 0))
    def _():
        run([(0, own, *load(own, q0, g0), st0[own]), (1, sib, *load(sib, q1, g1), st1[sib])])

    @pl.when((own >= 0) != (sib >= 0))
    def _():
        block = jnp.maximum(own, sib)
        side = jnp.where(own >= 0, 0, 1)

        @pl.when(side == 0)
        def _():
            q_buf[...], g_buf[...] = load(block, q0, g0)

        @pl.when(side == 1)
        def _():
            q_buf[...], g_buf[...] = load(block, q1, g1)

        stats = jnp.where(side == 0, st0[block], st1[block])
        run([(side, block, q_buf[...], g_buf[...], stats)])

    @pl.when((own < 0) & (sib < 0))
    def _():
        buf[...] = jnp.zeros_like(buf)

    for i, out_ref in enumerate(outs):

        @pl.when(at // SIDE == i)
        def _():
            out_ref[0] = buf[...]

    @pl.when(at == pl.num_programs(0) - 1)
    def _():
        out0[...] = dq[0].astype(out0.dtype)
        out1[...] = dq[1].astype(out1.dtype)


def remote_grads(table, own, sib, stats, groups, bases, scale2):
    heads, _, width = own.shape
    rows = stats[0].shape[0] * QB
    count = len(bases)
    once = pl.Buffered(1)
    q_spec = pl.BlockSpec((heads, rows, width), lambda k, t: (0, 0, 0), pipeline_mode=once)
    g_spec = pl.BlockSpec((heads, rows, width), lambda k, t: (0, 1, 0), pipeline_mode=once)
    stat = pl.BlockSpec(stats[0].shape, lambda k, t: (0, 0, 0))
    acc_spec = pl.BlockSpec((heads, rows, width), lambda k, t: (0, 0, 0))

    def piece(start, size):
        return pl.BlockSpec(
            (1, 2, rows, width), lambda k, t: (jnp.clip(k - start, 0, size - 1), 0, 0, 0)
        )

    operands = [array for group in groups for array in group]
    offsets = [0]
    for array in operands:
        offsets.append(offsets[-1] + array.shape[0])
    acc = jax.ShapeDtypeStruct((heads, rows, width), jnp.bfloat16)
    part = jax.ShapeDtypeStruct((SIDE, 2, rows, width), jnp.bfloat16)
    return pl.pallas_call(
        functools.partial(remote_kernel, scale2, bases, offsets),
        grid_spec=pltpu.PrefetchScalarGridSpec(
            num_scalar_prefetch=1,
            grid=(SIDE * count,),
            in_specs=[q_spec, g_spec, q_spec, g_spec, stat, stat]
            + [piece(start, array.shape[0]) for start, array in zip(offsets, operands)],
            out_specs=[acc_spec, acc_spec] + [piece(SIDE * i, SIDE) for i in range(count)],
            scratch_shapes=[
                pltpu.VMEM((2, rows, width), jnp.bfloat16),
                pltpu.VMEM((heads * QB, width), jnp.bfloat16),
                pltpu.VMEM((heads * QB, width), jnp.bfloat16),
                pltpu.VMEM((2, heads, rows, width), jnp.float32),
            ],
        ),
        out_shape=[acc, acc] + [part] * count,
        compiler_params=pltpu.CompilerParams(vmem_limit_bytes=VMEM_LIMIT),
        cost_estimate=pl.CostEstimate(
            flops=SIDE * count * 10 * heads * QB * rows * width,
            bytes_accessed=(8 + 4 * count) << 20,
            transcendentals=0,
        ),
        name="remote",
    )(table, own, own, sib, sib, *stats, *operands)


def split3(value):
    terms = []
    for _ in range(3):
        term = lax.reduce_precision(value, 8, 7)
        terms.append(term.astype(jnp.bfloat16))
        value = value - term
    return jnp.stack(terms, axis=-2)


def grads(queries, key_rows, value_rows, out_grad, outputs, logsumexp, selections):
    rows, kv_heads, _, width = queries.shape
    blocks = rows // QB
    scale = width ** (-0.5)
    scale2 = scale * LOG2E
    me = lax.axis_index("ctx")
    head = lax.axis_index("head")
    x, z, core = me // (2 * SIDE), (me // 2) % SIDE, me % 2

    keys = lax.dynamic_index_in_dim(key_rows, head, 1, keepdims=False)
    values = lax.dynamic_index_in_dim(value_rows, head, 1, keepdims=False)
    both = jnp.stack([keys, values])
    behind = shift(both, 0, 1)
    ahead = shift(both, 0, -1)
    across = shift(both, 0, 2)
    sides = jnp.stack([behind, ahead])
    line = (both[None], sides, across[None])
    line_behind = tuple(shift(piece, 1, 1) for piece in line)
    line_ahead = tuple(shift(piece, 1, -1) for piece in line)
    line_across = (
        shift(line_behind[0], 1, 1), shift(line_ahead[1], 1, -1), shift(line_behind[2], 1, 1)
    )

    def turn(value):
        return lax.all_to_all(value, "head", split_axis=0, concat_axis=0, tiled=True)

    delta = jnp.sum(out_grad.astype(jnp.float32) * outputs.astype(jnp.float32), axis=-1)
    stats = jnp.stack([logsumexp[:, 0] * LOG2E, delta[:, :, 0].T], axis=1)
    stats = split3(stats.reshape(kv_heads, 2, rows)).reshape(kv_heads, -1, width)
    own = turn(
        jnp.concatenate(
            [
                jnp.transpose(queries[:, :, 0], (1, 0, 2)),
                jnp.transpose(out_grad[:, :, 0], (1, 0, 2)),
                stats,
            ],
            axis=1,
        ),
    )
    sib = other_core(own)
    sib_selections = other_core(selections)

    def stats_of(packed):
        terms = packed[:, 2 * rows :].reshape(-1, 2, 3, blocks, QB).astype(jnp.float32)
        return (terms[:, :, 0] + terms[:, :, 1] + terms[:, :, 2]).transpose(2, 1, 0, 3).reshape(blocks, 2, -1)

    own_stats, sib_stats = stats_of(own), stats_of(sib)

    index = jnp.arange(SIDE * SIDE, dtype=jnp.int32)
    near, far = index % SIDE, index // SIDE
    near = jnp.where(near >= 2, 5 - near, near)
    back_x, back_z = jnp.where(core == 0, near, far), jnp.where(core == 0, far, near)
    source = (((x - back_x) % SIDE) * SIDE + (z - back_z) % SIDE) * 2 + core

    def listed(picks, device):
        hit = ((picks[:, 1:2] == source) | (picks[:, 2:3] == source)) & (source != device)
        return jnp.max(jnp.where(hit, jnp.arange(blocks, dtype=jnp.int32)[:, None], -1), axis=0)

    table = jnp.concatenate([listed(selections, me), listed(sib_selections, me + 1 - 2 * core)])

    def remote(groups, bases):
        return remote_grads(table, own, sib, (own_stats, sib_stats), groups, bases, scale2)

    level0, level1, part_line = remote([line], (0,))
    first0, first1, part_behind, part_ahead = remote([line_behind, line_ahead], (SIDE, 3 * SIDE))
    back_behind = shift(part_behind, 1, -1)
    back_ahead = shift(part_ahead, 1, 1)
    second0, second1, part_across = remote([line_across], (2 * SIDE,))
    back_across = shift(part_across, 1, 2)
    own_q, own_k, own_v = own_grads(own, own_stats, keys, values, scale2)

    def summed(*parts):
        return sum(part.astype(jnp.float32) for part in parts)

    total = [
        summed(part_line[i], back_behind[i], back_ahead[i], back_across[i])
        for i in range(SIDE)
    ]
    low = [part.astype(jnp.bfloat16) for part in total[1:]]
    near_sum = (
        total[0]
        + shift(low[0], 0, -1).astype(jnp.float32)
        + shift(low[1], 0, 1).astype(jnp.float32)
        + shift(low[2], 0, 2).astype(jnp.float32)
    )
    grad_k = ((near_sum[0] + own_k) * scale).astype(jnp.bfloat16)
    grad_v = (near_sum[1] + own_v).astype(jnp.bfloat16)

    dq_low = summed(level1, first1, second1).astype(jnp.bfloat16)
    returned = other_core(dq_low)
    dq = ((own_q + summed(level0, first0, second0, returned)) * scale).astype(jnp.bfloat16)
    dq = jnp.transpose(turn(dq), (1, 0, 2))[:, :, None]
    return dq, grad_k[:, None], grad_v[:, None]


def solution(mesh):
    in_specs = (
        P("ctx", None, "head", None),
        P("ctx", None, None),
        P("ctx", None, None),
        P("ctx", None, "head", None),
        P("ctx", None, "head", None),
        P(None, "head", "ctx"),
        P("ctx", None),
    )
    out_specs = (P("ctx", None, "head", None), P("ctx", "head", None), P("ctx", "head", None))
    return jax.shard_map(grads, mesh=mesh, in_specs=in_specs, out_specs=out_specs, check_vma=False)
```

```python
import functools
import math

import jax
import jax.numpy as jnp
from jax import lax
from jax.experimental import pallas as pl
from jax.experimental.pallas import tpu as pltpu
from jax.sharding import PartitionSpec as P


QB = 128
SIDE = 4
OWN_TILE = 512
VMEM_LIMIT = 60 * 1024 * 1024
LOG2E = math.log2(math.e)


NT = (((1,), (1,)), ((), ()))
NN = (((1,), (0,)), ((), ()))
TN = (((0,), (0,)), ((), ()))


def dot(a, b, dims):
    return lax.dot_general(a, b, dims, preferred_element_type=jnp.float32)


def pairs(place):
    found = []
    for x in range(SIDE):
        for z in range(SIDE):
            for core in range(2):
                to_x, to_z, to_core = place(x, z, core)
                target = (to_x % SIDE * SIDE + to_z % SIDE) * 2 + to_core
                found.append(((x * SIDE + z) * 2 + core, target))
    return found


def shift(value, phase, step):
    def place(x, z, core):
        along_x = step if core == phase else 0
        return x + along_x, z + step - along_x, core

    return lax.ppermute(value, "ctx", pairs(place))


def other_core(value):
    return lax.ppermute(value, "ctx", pairs(lambda x, z, core: (x, z, 1 - core)))


def tile_grads(keys, values, q, g, lse, delta, scale2, mask=None):
    prob = jnp.exp2(dot(keys, q, NT) * scale2 - lse)
    if mask is not None:
        prob = jnp.where(mask, prob, 0.0)
    dscore = prob * (dot(values, g, NT) - delta)
    prob_low = prob.astype(jnp.bfloat16)
    dscore_low = dscore.astype(jnp.bfloat16)
    return dot(dscore_low, q, NN), dot(prob_low, g, NN), dot(dscore_low, keys, TN)


def own_kernel(scale2, q_ref, g_ref, st_ref, k_ref, v_ref, dq_ref, dk_ref, dv_ref):
    block = pl.program_id(0)

    @pl.when(block == 0)
    def _():
        dk_ref[...] = jnp.zeros_like(dk_ref)
        dv_ref[...] = jnp.zeros_like(dv_ref)

    rows = q_ref.shape[0] * QB
    q = q_ref[...].reshape(rows, -1)
    g = g_ref[...].reshape(rows, -1)
    lse = st_ref[0, 0:1, :]
    delta = st_ref[0, 1:2, :]
    ahead = lax.broadcasted_iota(jnp.int32, (OWN_TILE, rows), 0) - (
        lax.broadcasted_iota(jnp.int32, (OWN_TILE, rows), 1) & (QB - 1)
    )

    def step(tile, masked):
        where = pl.ds(tile * OWN_TILE, OWN_TILE)
        mask = ahead <= block * QB - tile * OWN_TILE if masked else None
        dk, dv, dq = tile_grads(
            k_ref[where, :], v_ref[where, :], q, g, lse, delta, scale2, mask
        )
        dk_ref[where, :] += dk
        dv_ref[where, :] += dv
        return dq

    reach = OWN_TILE // QB
    for last in range(k_ref.shape[0] // OWN_TILE):

        @pl.when(block // reach == last)
        def _():
            dq = step(last, True)
            for tile in range(last):
                dq += step(tile, False)
            dq_ref[...] = dq.reshape(dq_ref.shape)


def own_grads(packed, stats, keys, values, scale2):
    heads, _, width = packed.shape
    rows = keys.shape[0]
    blocks = rows // QB
    q_spec = pl.BlockSpec((heads, QB, width), lambda b: (0, b, 0))
    g_spec = pl.BlockSpec((heads, QB, width), lambda b: (0, b + blocks, 0))
    whole = pl.BlockSpec((rows, width), lambda b: (0, 0))
    acc = jax.ShapeDtypeStruct(keys.shape, jnp.float32)
    return pl.pallas_call(
        functools.partial(own_kernel, scale2),
        grid=(blocks,),
        in_specs=[q_spec, g_spec, pl.BlockSpec((1, 2, heads * QB), lambda b: (b, 0, 0)), whole, whole],
        out_specs=[q_spec, whole, whole],
        out_shape=[jax.ShapeDtypeStruct((heads, rows, width), jnp.float32), acc, acc],
        compiler_params=pltpu.CompilerParams(vmem_limit_bytes=VMEM_LIMIT),
        cost_estimate=pl.CostEstimate(
            flops=6 * heads * rows * rows * width, bytes_accessed=8 << 20, transcendentals=0
        ),
        name="own",
    )(packed, packed, stats, keys, values)


def remote_kernel(scale2, bases, offsets, tbl, *refs):
    sources = len(offsets) - 1
    q0, g0, q1, g1, st0, st1 = refs[:6]
    blocks = refs[6 : 6 + sources]
    out0, out1 = refs[6 + sources : 8 + sources]
    outs = refs[8 + sources : -4]
    buf, q_buf, g_buf, dq = refs[-4:]
    at = pl.program_id(0)
    heads = q0.shape[0]
    rows = heads * QB

    @pl.when(at == 0)
    def _():
        dq[...] = jnp.zeros_like(dq)

    for i, block_ref in enumerate(blocks):

        @pl.when((at >= offsets[i]) & (at < offsets[i + 1]))
        def _():
            buf[...] = block_ref[0]

    entry = at % SIDE + bases[0]
    for i in range(1, len(bases)):
        entry = jnp.where(at // SIDE == i, at % SIDE + bases[i], entry)
    own = tbl[entry]
    sib = tbl[SIDE * SIDE + entry]

    def rows_of(block):
        return pl.ds(pl.multiple_of(block * QB, QB), QB)

    def load(block, q_ref, g_ref):
        where = rows_of(block)
        return q_ref[:, where, :].reshape(rows, -1), g_ref[:, where, :].reshape(rows, -1)

    def run(units):
        dk_sum, dv_sum = None, None
        for side, block, q, g, stats in units:
            dk, dv, dq_part = tile_grads(
                buf[0], buf[1], q, g, stats[0:1, :], stats[1:2, :], scale2
            )
            dk_sum = dk if dk_sum is None else dk_sum + dk
            dv_sum = dv if dv_sum is None else dv_sum + dv
            dq[side, :, rows_of(block), :] += dq_part.reshape(heads, QB, -1)
        buf[0] = dk_sum.astype(jnp.bfloat16)
        buf[1] = dv_sum.astype(jnp.bfloat16)

    @pl.when((own >= 0) & (sib >= 0))
    def _():
        run([(0, own, *load(own, q0, g0), st0[own]), (1, sib, *load(sib, q1, g1), st1[sib])])

    @pl.when((own >= 0) != (sib >= 0))
    def _():
        block = jnp.maximum(own, sib)
        side = jnp.where(own >= 0, 0, 1)

        @pl.when(side == 0)
        def _():
            q_buf[...], g_buf[...] = load(block, q0, g0)

        @pl.when(side == 1)
        def _():
            q_buf[...], g_buf[...] = load(block, q1, g1)

        stats = jnp.where(side == 0, st0[block], st1[block])
        run([(side, block, q_buf[...], g_buf[...], stats)])

    @pl.when((own < 0) & (sib < 0))
    def _():
        buf[...] = jnp.zeros_like(buf)

    for i, out_ref in enumerate(outs):

        @pl.when(at // SIDE == i)
        def _():
            out_ref[0] = buf[...]

    @pl.when(at == pl.num_programs(0) - 1)
    def _():
        out0[...] = dq[0].astype(out0.dtype)
        out1[...] = dq[1].astype(out1.dtype)


def remote_grads(table, own, sib, stats, groups, bases, scale2):
    heads, _, width = own.shape
    rows = stats[0].shape[0] * QB
    count = len(bases)
    once = pl.Buffered(1)
    q_spec = pl.BlockSpec((heads, rows, width), lambda k, t: (0, 0, 0), pipeline_mode=once)
    g_spec = pl.BlockSpec((heads, rows, width), lambda k, t: (0, 1, 0), pipeline_mode=once)
    stat = pl.BlockSpec(stats[0].shape, lambda k, t: (0, 0, 0))
    acc_spec = pl.BlockSpec((heads, rows, width), lambda k, t: (0, 0, 0))

    def piece(start, size):
        return pl.BlockSpec(
            (1, 2, rows, width), lambda k, t: (jnp.clip(k - start, 0, size - 1), 0, 0, 0)
        )

    operands = [array for group in groups for array in group]
    offsets = [0]
    for array in operands:
        offsets.append(offsets[-1] + array.shape[0])
    acc = jax.ShapeDtypeStruct((heads, rows, width), jnp.bfloat16)
    part = jax.ShapeDtypeStruct((SIDE, 2, rows, width), jnp.bfloat16)
    return pl.pallas_call(
        functools.partial(remote_kernel, scale2, bases, offsets),
        grid_spec=pltpu.PrefetchScalarGridSpec(
            num_scalar_prefetch=1,
            grid=(SIDE * count,),
            in_specs=[q_spec, g_spec, q_spec, g_spec, stat, stat]
            + [piece(start, array.shape[0]) for start, array in zip(offsets, operands)],
            out_specs=[acc_spec, acc_spec] + [piece(SIDE * i, SIDE) for i in range(count)],
            scratch_shapes=[
                pltpu.VMEM((2, rows, width), jnp.bfloat16),
                pltpu.VMEM((heads * QB, width), jnp.bfloat16),
                pltpu.VMEM((heads * QB, width), jnp.bfloat16),
                pltpu.VMEM((2, heads, rows, width), jnp.float32),
            ],
        ),
        out_shape=[acc, acc] + [part] * count,
        compiler_params=pltpu.CompilerParams(vmem_limit_bytes=VMEM_LIMIT),
        cost_estimate=pl.CostEstimate(
            flops=SIDE * count * 10 * heads * QB * rows * width,
            bytes_accessed=(8 + 4 * count) << 20,
            transcendentals=0,
        ),
        name="remote",
    )(table, own, own, sib, sib, *stats, *operands)


def split3(value):
    terms = []
    for _ in range(3):
        term = lax.reduce_precision(value, 8, 7)
        terms.append(term.astype(jnp.bfloat16))
        value = value - term
    return jnp.stack(terms, axis=-2)


def grads(queries, key_rows, value_rows, out_grad, outputs, logsumexp, selections):
    rows, kv_heads, _, width = queries.shape
    blocks = rows // QB
    scale = width ** (-0.5)
    scale2 = scale * LOG2E
    me = lax.axis_index("ctx")
    head = lax.axis_index("head")
    x, z, core = me // (2 * SIDE), (me // 2) % SIDE, me % 2

    keys = lax.dynamic_index_in_dim(key_rows, head, 1, keepdims=False)
    values = lax.dynamic_index_in_dim(value_rows, head, 1, keepdims=False)
    both = jnp.stack([keys, values])
    behind = shift(both, 0, 1)
    ahead = shift(both, 0, -1)
    across = shift(both, 0, 2)
    sides = jnp.stack([behind, ahead])
    line = (both[None], sides, across[None])
    line_behind = tuple(shift(piece, 1, 1) for piece in line)
    line_ahead = tuple(shift(piece, 1, -1) for piece in line)
    line_across = (
        shift(line_behind[0], 1, 1), shift(line_ahead[1], 1, -1), shift(line_behind[2], 1, 1)
    )

    def turn(value):
        return lax.all_to_all(value, "head", split_axis=0, concat_axis=0, tiled=True)

    delta = jnp.sum(out_grad.astype(jnp.float32) * outputs.astype(jnp.float32), axis=-1)
    stats = jnp.stack([logsumexp[:, 0] * LOG2E, delta[:, :, 0].T], axis=1)
    stats = split3(stats.reshape(kv_heads, 2, rows)).reshape(kv_heads, -1, width)
    own = turn(
        jnp.concatenate(
            [
                jnp.transpose(queries[:, :, 0], (1, 0, 2)),
                jnp.transpose(out_grad[:, :, 0], (1, 0, 2)),
                stats,
            ],
            axis=1,
        ),
    )
    sib = other_core(own)
    sib_selections = other_core(selections)

    def stats_of(packed):
        terms = packed[:, 2 * rows :].reshape(-1, 2, 3, blocks, QB).astype(jnp.float32)
        return (terms[:, :, 0] + terms[:, :, 1] + terms[:, :, 2]).transpose(2, 1, 0, 3).reshape(blocks, 2, -1)

    own_stats, sib_stats = stats_of(own), stats_of(sib)

    index = jnp.arange(SIDE * SIDE, dtype=jnp.int32)
    near, far = index % SIDE, index // SIDE
    near = jnp.where(near >= 2, 5 - near, near)
    back_x, back_z = jnp.where(core == 0, near, far), jnp.where(core == 0, far, near)
    source = (((x - back_x) % SIDE) * SIDE + (z - back_z) % SIDE) * 2 + core

    def listed(picks, device):
        hit = ((picks[:, 1:2] == source) | (picks[:, 2:3] == source)) & (source != device)
        return jnp.max(jnp.where(hit, jnp.arange(blocks, dtype=jnp.int32)[:, None], -1), axis=0)

    table = jnp.concatenate([listed(selections, me), listed(sib_selections, me + 1 - 2 * core)])

    def remote(groups, bases):
        return remote_grads(table, own, sib, (own_stats, sib_stats), groups, bases, scale2)

    level0, level1, part_line = remote([line], (0,))
    first0, first1, part_behind, part_ahead = remote([line_behind, line_ahead], (SIDE, 3 * SIDE))
    back_behind = shift(part_behind, 1, -1)
    back_ahead = shift(part_ahead, 1, 1)
    second0, second1, part_across = remote([line_across], (2 * SIDE,))
    own_q, own_k, own_v = own_grads(own, own_stats, keys, values, scale2)

    def summed(*parts):
        return sum(part.astype(jnp.float32) for part in parts)

    def spread(parts):
        return (shift(parts[0], 0, -1), shift(parts[1], 0, 1), shift(parts[2], 0, 2))

    side = spread(part_across[1:])
    far_sum = summed(part_across[0], *side).astype(jnp.bfloat16)
    total = [summed(part_line[i], back_behind[i], back_ahead[i]) for i in range(SIDE)]
    received = spread([part.astype(jnp.bfloat16) for part in total[1:]])
    received += (shift(far_sum, 1, 2),)

    def final(i, own_part, factor):
        return ((total[0][i] + summed(*(part[i] for part in received)) + own_part) * factor).astype(
            jnp.bfloat16
        )

    grad_k, grad_v = final(0, own_k, scale), final(1, own_v, 1.0)

    dq_low = summed(level1, first1, second1).astype(jnp.bfloat16)
    returned = other_core(dq_low)
    dq = ((own_q + summed(level0, first0, second0, returned)) * scale).astype(jnp.bfloat16)
    dq = jnp.transpose(turn(dq), (1, 0, 2))[:, :, None]
    return dq, grad_k[:, None], grad_v[:, None]


def solution(mesh):
    in_specs = (
        P("ctx", None, "head", None),
        P("ctx", None, None),
        P("ctx", None, None),
        P("ctx", None, "head", None),
        P("ctx", None, "head", None),
        P(None, "head", "ctx"),
        P("ctx", None),
    )
    out_specs = (P("ctx", None, "head", None), P("ctx", "head", None), P("ctx", "head", None))
    return jax.shard_map(grads, mesh=mesh, in_specs=in_specs, out_specs=out_specs, check_vma=False)
```

```python
import functools
import math

import jax
import jax.numpy as jnp
from jax import lax
from jax.experimental import pallas as pl
from jax.experimental.pallas import tpu as pltpu
from jax.sharding import PartitionSpec as P


QB = 128
SIDE = 4
OWN_TILE = 512
VMEM_LIMIT = 60 * 1024 * 1024
LOG2E = math.log2(math.e)


NT = (((1,), (1,)), ((), ()))
NN = (((1,), (0,)), ((), ()))
TN = (((0,), (0,)), ((), ()))


def dot(a, b, dims):
    return lax.dot_general(a, b, dims, preferred_element_type=jnp.float32)


def pairs(place):
    found = []
    for x in range(SIDE):
        for z in range(SIDE):
            for core in range(2):
                to_x, to_z, to_core = place(x, z, core)
                target = (to_x % SIDE * SIDE + to_z % SIDE) * 2 + to_core
                found.append(((x * SIDE + z) * 2 + core, target))
    return found


def shift(value, phase, step):
    def place(x, z, core):
        along_x = step if core == phase else 0
        return x + along_x, z + step - along_x, core

    return lax.ppermute(value, "ctx", pairs(place))


def other_core(value):
    return lax.ppermute(value, "ctx", pairs(lambda x, z, core: (x, z, 1 - core)))


def tile_grads(keys, values, q, g, lse, delta, scale2, mask=None):
    prob = jnp.exp2(dot(keys, q, NT) * scale2 - lse)
    if mask is not None:
        prob = jnp.where(mask, prob, 0.0)
    dscore = prob * (dot(values, g, NT) - delta)
    prob_low = prob.astype(jnp.bfloat16)
    dscore_low = dscore.astype(jnp.bfloat16)
    return dot(dscore_low, q, NN), dot(prob_low, g, NN), dot(dscore_low, keys, TN)


def own_kernel(scale2, q_ref, g_ref, st_ref, k_ref, v_ref, dq_ref, dk_ref, dv_ref):
    block = pl.program_id(0)

    @pl.when(block == 0)
    def _():
        dk_ref[...] = jnp.zeros_like(dk_ref)
        dv_ref[...] = jnp.zeros_like(dv_ref)

    rows = q_ref.shape[0] * QB
    q = q_ref[...].reshape(rows, -1)
    g = g_ref[...].reshape(rows, -1)
    lse = st_ref[0, 0:1, :]
    delta = st_ref[0, 1:2, :]
    ahead = lax.broadcasted_iota(jnp.int32, (OWN_TILE, rows), 0) - (
        lax.broadcasted_iota(jnp.int32, (OWN_TILE, rows), 1) & (QB - 1)
    )

    def step(tile, masked):
        where = pl.ds(tile * OWN_TILE, OWN_TILE)
        mask = ahead <= block * QB - tile * OWN_TILE if masked else None
        dk, dv, dq = tile_grads(
            k_ref[where, :], v_ref[where, :], q, g, lse, delta, scale2, mask
        )
        dk_ref[where, :] += dk
        dv_ref[where, :] += dv
        return dq

    reach = OWN_TILE // QB
    for last in range(k_ref.shape[0] // OWN_TILE):

        @pl.when(block // reach == last)
        def _():
            dq = step(last, True)
            for tile in range(last):
                dq += step(tile, False)
            dq_ref[...] = dq.reshape(dq_ref.shape)


def own_grads(packed, stats, keys, values, scale2):
    heads, _, width = packed.shape
    rows = keys.shape[0]
    blocks = rows // QB
    q_spec = pl.BlockSpec((heads, QB, width), lambda b: (0, b, 0))
    g_spec = pl.BlockSpec((heads, QB, width), lambda b: (0, b + blocks, 0))
    whole = pl.BlockSpec((rows, width), lambda b: (0, 0))
    acc = jax.ShapeDtypeStruct(keys.shape, jnp.float32)
    return pl.pallas_call(
        functools.partial(own_kernel, scale2),
        grid=(blocks,),
        in_specs=[q_spec, g_spec, pl.BlockSpec((1, 2, heads * QB), lambda b: (b, 0, 0)), whole, whole],
        out_specs=[q_spec, whole, whole],
        out_shape=[jax.ShapeDtypeStruct((heads, rows, width), jnp.float32), acc, acc],
        compiler_params=pltpu.CompilerParams(vmem_limit_bytes=VMEM_LIMIT),
        cost_estimate=pl.CostEstimate(
            flops=6 * heads * rows * rows * width, bytes_accessed=8 << 20, transcendentals=0
        ),
        name="own",
    )(packed, packed, stats, keys, values)


def remote_kernel(scale2, bases, offsets, out_offsets, tbl, *refs):
    sources = len(offsets) - 1
    q0, g0, q1, g1, st0, st1 = refs[:6]
    blocks = refs[6 : 6 + sources]
    out0, out1 = refs[6 + sources : 8 + sources]
    outs = refs[8 + sources : -4]
    buf, q_buf, g_buf, dq = refs[-4:]
    at = pl.program_id(0)
    heads = q0.shape[0]
    rows = heads * QB

    @pl.when(at == 0)
    def _():
        dq[...] = jnp.zeros_like(dq)

    for i, block_ref in enumerate(blocks):

        @pl.when((at >= offsets[i]) & (at < offsets[i + 1]))
        def _():
            buf[...] = block_ref[0]

    entry = at % SIDE + bases[0]
    for i in range(1, len(bases)):
        entry = jnp.where(at // SIDE == i, at % SIDE + bases[i], entry)
    own = tbl[entry]
    sib = tbl[SIDE * SIDE + entry]

    def rows_of(block):
        return pl.ds(pl.multiple_of(block * QB, QB), QB)

    def load(block, q_ref, g_ref):
        where = rows_of(block)
        return q_ref[:, where, :].reshape(rows, -1), g_ref[:, where, :].reshape(rows, -1)

    def run(units):
        dk_sum, dv_sum = None, None
        for side, block, q, g, stats in units:
            dk, dv, dq_part = tile_grads(
                buf[0], buf[1], q, g, stats[0:1, :], stats[1:2, :], scale2
            )
            dk_sum = dk if dk_sum is None else dk_sum + dk
            dv_sum = dv if dv_sum is None else dv_sum + dv
            dq[side, :, rows_of(block), :] += dq_part.reshape(heads, QB, -1)
        buf[0] = dk_sum.astype(jnp.bfloat16)
        buf[1] = dv_sum.astype(jnp.bfloat16)

    @pl.when((own >= 0) & (sib >= 0))
    def _():
        run([(0, own, *load(own, q0, g0), st0[own]), (1, sib, *load(sib, q1, g1), st1[sib])])

    @pl.when((own >= 0) != (sib >= 0))
    def _():
        block = jnp.maximum(own, sib)
        side = jnp.where(own >= 0, 0, 1)

        @pl.when(side == 0)
        def _():
            q_buf[...], g_buf[...] = load(block, q0, g0)

        @pl.when(side == 1)
        def _():
            q_buf[...], g_buf[...] = load(block, q1, g1)

        stats = jnp.where(side == 0, st0[block], st1[block])
        run([(side, block, q_buf[...], g_buf[...], stats)])

    @pl.when((own < 0) & (sib < 0))
    def _():
        buf[...] = jnp.zeros_like(buf)

    for i, out_ref in enumerate(outs):

        @pl.when((at >= out_offsets[i]) & (at < out_offsets[i + 1]))
        def _():
            out_ref[0] = buf[...]

    @pl.when(at == pl.num_programs(0) - 1)
    def _():
        out0[...] = dq[0].astype(out0.dtype)
        out1[...] = dq[1].astype(out1.dtype)


def remote_grads(table, own, sib, stats, groups, bases, out_sizes, scale2):
    heads, _, width = own.shape
    rows = stats[0].shape[0] * QB
    count = len(bases)
    once = pl.Buffered(1)
    q_spec = pl.BlockSpec((heads, rows, width), lambda k, t: (0, 0, 0), pipeline_mode=once)
    g_spec = pl.BlockSpec((heads, rows, width), lambda k, t: (0, 1, 0), pipeline_mode=once)
    stat = pl.BlockSpec(stats[0].shape, lambda k, t: (0, 0, 0))
    acc_spec = pl.BlockSpec((heads, rows, width), lambda k, t: (0, 0, 0))

    def piece(start, size):
        return pl.BlockSpec(
            (1, 2, rows, width), lambda k, t: (jnp.clip(k - start, 0, size - 1), 0, 0, 0)
        )

    operands = [array for group in groups for array in group]
    offsets = [0]
    for array in operands:
        offsets.append(offsets[-1] + array.shape[0])
    out_offsets = [0]
    for size in out_sizes:
        out_offsets.append(out_offsets[-1] + size)
    acc = jax.ShapeDtypeStruct((heads, rows, width), jnp.bfloat16)
    return pl.pallas_call(
        functools.partial(remote_kernel, scale2, bases, offsets, out_offsets),
        grid_spec=pltpu.PrefetchScalarGridSpec(
            num_scalar_prefetch=1,
            grid=(SIDE * count,),
            in_specs=[q_spec, g_spec, q_spec, g_spec, stat, stat]
            + [piece(start, array.shape[0]) for start, array in zip(offsets, operands)],
            out_specs=[acc_spec, acc_spec]
            + [piece(start, size) for start, size in zip(out_offsets, out_sizes)],
            scratch_shapes=[
                pltpu.VMEM((2, rows, width), jnp.bfloat16),
                pltpu.VMEM((heads * QB, width), jnp.bfloat16),
                pltpu.VMEM((heads * QB, width), jnp.bfloat16),
                pltpu.VMEM((2, heads, rows, width), jnp.float32),
            ],
        ),
        out_shape=[acc, acc]
        + [jax.ShapeDtypeStruct((size, 2, rows, width), jnp.bfloat16) for size in out_sizes],
        compiler_params=pltpu.CompilerParams(vmem_limit_bytes=VMEM_LIMIT),
        cost_estimate=pl.CostEstimate(
            flops=SIDE * count * 10 * heads * QB * rows * width,
            bytes_accessed=(8 + 4 * count) << 20,
            transcendentals=0,
        ),
        name="remote",
    )(table, own, own, sib, sib, *stats, *operands)


def split3(value):
    terms = []
    for _ in range(3):
        term = lax.reduce_precision(value, 8, 7)
        terms.append(term.astype(jnp.bfloat16))
        value = value - term
    return jnp.stack(terms, axis=-2)


def grads(queries, key_rows, value_rows, out_grad, outputs, logsumexp, selections):
    rows, kv_heads, _, width = queries.shape
    blocks = rows // QB
    scale = width ** (-0.5)
    scale2 = scale * LOG2E
    me = lax.axis_index("ctx")
    head = lax.axis_index("head")
    x, z, core = me // (2 * SIDE), (me // 2) % SIDE, me % 2

    keys = lax.dynamic_index_in_dim(key_rows, head, 1, keepdims=False)
    values = lax.dynamic_index_in_dim(value_rows, head, 1, keepdims=False)
    both = jnp.stack([keys, values])
    behind = shift(both, 0, 1)
    ahead = shift(both, 0, -1)
    across = shift(both, 0, 2)
    sides = jnp.stack([behind, ahead])
    line = (both[None], sides, across[None])
    line_behind = tuple(shift(piece, 1, 1) for piece in line)
    line_ahead = tuple(shift(piece, 1, -1) for piece in line)
    line_across = (
        shift(line_behind[0], 1, 1), shift(line_ahead[1], 1, -1), shift(line_behind[2], 1, 1)
    )

    def turn(value):
        return lax.all_to_all(value, "head", split_axis=0, concat_axis=0, tiled=True)

    delta = jnp.sum(out_grad.astype(jnp.float32) * outputs.astype(jnp.float32), axis=-1)
    stats = jnp.stack([logsumexp[:, 0] * LOG2E, delta[:, :, 0].T], axis=1)
    stats = split3(stats.reshape(kv_heads, 2, rows)).reshape(kv_heads, -1, width)
    own = turn(
        jnp.concatenate(
            [
                jnp.transpose(queries[:, :, 0], (1, 0, 2)),
                jnp.transpose(out_grad[:, :, 0], (1, 0, 2)),
                stats,
            ],
            axis=1,
        ),
    )
    sib = other_core(own)
    sib_selections = other_core(selections)

    def stats_of(packed):
        terms = packed[:, 2 * rows :].reshape(-1, 2, 3, blocks, QB).astype(jnp.float32)
        return (terms[:, :, 0] + terms[:, :, 1] + terms[:, :, 2]).transpose(2, 1, 0, 3).reshape(blocks, 2, -1)

    own_stats, sib_stats = stats_of(own), stats_of(sib)

    index = jnp.arange(SIDE * SIDE, dtype=jnp.int32)
    near, far = index % SIDE, index // SIDE
    near = jnp.where(near >= 2, 5 - near, near)
    back_x, back_z = jnp.where(core == 0, near, far), jnp.where(core == 0, far, near)
    source = (((x - back_x) % SIDE) * SIDE + (z - back_z) % SIDE) * 2 + core

    def listed(picks, device):
        hit = ((picks[:, 1:2] == source) | (picks[:, 2:3] == source)) & (source != device)
        return jnp.max(jnp.where(hit, jnp.arange(blocks, dtype=jnp.int32)[:, None], -1), axis=0)

    table = jnp.concatenate([listed(selections, me), listed(sib_selections, me + 1 - 2 * core)])

    def remote(groups, bases, out_sizes):
        return remote_grads(
            table, own, sib, (own_stats, sib_stats), groups, bases, out_sizes, scale2
        )

    first0, first1, part_behind, part_ahead = remote(
        [line_behind, line_ahead], (SIDE, 3 * SIDE), (SIDE, SIDE)
    )
    back_behind = shift(part_behind, 1, -1)
    back_ahead = shift(part_ahead, 1, 1)
    second0, second1, *part_across, part_line = remote(
        [line_across, line], (2 * SIDE, 0), (1,) * SIDE + (SIDE,)
    )
    part_across = [part[0] for part in part_across]
    own_q, own_k, own_v = own_grads(own, own_stats, keys, values, scale2)

    def summed(*parts):
        return sum(part.astype(jnp.float32) for part in parts)

    def spread(parts):
        return (shift(parts[0], 0, -1), shift(parts[1], 0, 1), shift(parts[2], 0, 2))

    side = spread(part_across[1:])
    far_sum = summed(part_across[0], *side).astype(jnp.bfloat16)
    total = [summed(part_line[i], back_behind[i], back_ahead[i]) for i in range(SIDE)]
    received = spread([part.astype(jnp.bfloat16) for part in total[1:]])
    received += (shift(far_sum, 1, 2),)

    def final(i, own_part, factor):
        return ((total[0][i] + summed(*(part[i] for part in received)) + own_part) * factor).astype(
            jnp.bfloat16
        )

    grad_k, grad_v = final(0, own_k, scale), final(1, own_v, 1.0)

    dq_low = summed(first1, second1).astype(jnp.bfloat16)
    returned = other_core(dq_low)
    dq = ((own_q + summed(first0, second0, returned)) * scale).astype(jnp.bfloat16)
    dq = jnp.transpose(turn(dq), (1, 0, 2))[:, :, None]
    return dq, grad_k[:, None], grad_v[:, None]


def solution(mesh):
    in_specs = (
        P("ctx", None, "head", None),
        P("ctx", None, None),
        P("ctx", None, None),
        P("ctx", None, "head", None),
        P("ctx", None, "head", None),
        P(None, "head", "ctx"),
        P("ctx", None),
    )
    out_specs = (P("ctx", None, "head", None), P("ctx", "head", None), P("ctx", "head", None))
    return jax.shard_map(grads, mesh=mesh, in_specs=in_specs, out_specs=out_specs, check_vma=False)
```

```python
import functools
import math

import jax
import jax.numpy as jnp
from jax import lax
from jax.experimental import pallas as pl
from jax.experimental.pallas import tpu as pltpu
from jax.sharding import PartitionSpec as P


QB = 128
SIDE = 4
OWN_TILE = 256
VMEM_LIMIT = 60 * 1024 * 1024
LOG2E = math.log2(math.e)


NT = (((1,), (1,)), ((), ()))
NN = (((1,), (0,)), ((), ()))
TN = (((0,), (0,)), ((), ()))


def dot(a, b, dims):
    return lax.dot_general(a, b, dims, preferred_element_type=jnp.float32)


def pairs(place):
    found = []
    for x in range(SIDE):
        for z in range(SIDE):
            for core in range(2):
                to_x, to_z, to_core = place(x, z, core)
                target = (to_x % SIDE * SIDE + to_z % SIDE) * 2 + to_core
                found.append(((x * SIDE + z) * 2 + core, target))
    return found


def shift(value, phase, step):
    def place(x, z, core):
        along_x = step if core == phase else 0
        return x + along_x, z + step - along_x, core

    return lax.ppermute(value, "ctx", pairs(place))


def other_core(value):
    return lax.ppermute(value, "ctx", pairs(lambda x, z, core: (x, z, 1 - core)))


def tile_grads(keys, values, q, g, lse, delta, scale2, mask=None):
    prob = jnp.exp2(dot(keys, q, NT) * scale2 - lse)
    if mask is not None:
        prob = jnp.where(mask, prob, 0.0)
    dscore = prob * (dot(values, g, NT) - delta)
    prob_low = prob.astype(jnp.bfloat16)
    dscore_low = dscore.astype(jnp.bfloat16)
    return dot(dscore_low, q, NN), dot(prob_low, g, NN), dot(dscore_low, keys, TN)


def own_kernel(scale2, q_ref, g_ref, st_ref, k_ref, v_ref, dq_ref, dk_ref, dv_ref):
    block = pl.program_id(0)

    @pl.when(block == 0)
    def _():
        dk_ref[...] = jnp.zeros_like(dk_ref)
        dv_ref[...] = jnp.zeros_like(dv_ref)

    rows = q_ref.shape[0] * QB
    q = q_ref[...].reshape(rows, -1)
    g = g_ref[...].reshape(rows, -1)
    lse = st_ref[0, 0:1, :]
    delta = st_ref[0, 1:2, :]
    ahead = lax.broadcasted_iota(jnp.int32, (OWN_TILE, rows), 0) - (
        lax.broadcasted_iota(jnp.int32, (OWN_TILE, rows), 1) & (QB - 1)
    )

    def step(tile, masked):
        where = pl.ds(tile * OWN_TILE, OWN_TILE)
        mask = ahead <= block * QB - tile * OWN_TILE if masked else None
        dk, dv, dq = tile_grads(
            k_ref[where, :], v_ref[where, :], q, g, lse, delta, scale2, mask
        )
        dk_ref[where, :] += dk
        dv_ref[where, :] += dv
        return dq

    reach = OWN_TILE // QB
    for last in range(k_ref.shape[0] // OWN_TILE):

        @pl.when(block // reach == last)
        def _():
            dq = step(last, True)
            for tile in range(last):
                dq += step(tile, False)
            dq_ref[...] = dq.reshape(dq_ref.shape)


def own_grads(packed, stats, keys, values, scale2):
    heads, _, width = packed.shape
    rows = keys.shape[0]
    blocks = rows // QB
    q_spec = pl.BlockSpec((heads, QB, width), lambda b: (0, b, 0))
    g_spec = pl.BlockSpec((heads, QB, width), lambda b: (0, b + blocks, 0))
    whole = pl.BlockSpec((rows, width), lambda b: (0, 0))
    acc = jax.ShapeDtypeStruct(keys.shape, jnp.float32)
    return pl.pallas_call(
        functools.partial(own_kernel, scale2),
        grid=(blocks,),
        in_specs=[q_spec, g_spec, pl.BlockSpec((1, 2, heads * QB), lambda b: (b, 0, 0)), whole, whole],
        out_specs=[q_spec, whole, whole],
        out_shape=[jax.ShapeDtypeStruct((heads, rows, width), jnp.float32), acc, acc],
        compiler_params=pltpu.CompilerParams(vmem_limit_bytes=VMEM_LIMIT),
        cost_estimate=pl.CostEstimate(
            flops=6 * heads * rows * rows * width, bytes_accessed=8 << 20, transcendentals=0
        ),
        name="own",
    )(packed, packed, stats, keys, values)


def remote_kernel(scale2, bases, offsets, out_offsets, fresh, tbl, *refs):
    sources = len(offsets) - 1
    q0, g0, q1, g1, st0, st1 = refs[:6]
    blocks = refs[6 : 6 + sources]
    rest = refs[6 + sources : -4]
    if not fresh:
        in0, in1, rest = rest[0], rest[1], rest[2:]
    out0, out1, outs = rest[0], rest[1], rest[2:]
    buf, q_buf, g_buf, dq = refs[-4:]
    at = pl.program_id(0)
    heads = q0.shape[0]
    rows = heads * QB

    @pl.when(at == 0)
    def _():
        if fresh:
            dq[...] = jnp.zeros_like(dq)
        else:
            dq[0] = in0[...].astype(jnp.float32)
            dq[1] = in1[...].astype(jnp.float32)

    for i, block_ref in enumerate(blocks):

        @pl.when((at >= offsets[i]) & (at < offsets[i + 1]))
        def _():
            buf[...] = block_ref[0]

    entry = at % SIDE + bases[0]
    for i in range(1, len(bases)):
        entry = jnp.where(at // SIDE == i, at % SIDE + bases[i], entry)
    own = tbl[entry]
    sib = tbl[SIDE * SIDE + entry]

    def rows_of(block):
        return pl.ds(pl.multiple_of(block * QB, QB), QB)

    def load(block, q_ref, g_ref):
        where = rows_of(block)
        return q_ref[:, where, :].reshape(rows, -1), g_ref[:, where, :].reshape(rows, -1)

    def run(units):
        dk_sum, dv_sum = None, None
        for side, block, q, g, stats in units:
            dk, dv, dq_part = tile_grads(
                buf[0], buf[1], q, g, stats[0:1, :], stats[1:2, :], scale2
            )
            dk_sum = dk if dk_sum is None else dk_sum + dk
            dv_sum = dv if dv_sum is None else dv_sum + dv
            dq[side, :, rows_of(block), :] += dq_part.reshape(heads, QB, -1)
        buf[0] = dk_sum.astype(jnp.bfloat16)
        buf[1] = dv_sum.astype(jnp.bfloat16)

    @pl.when((own >= 0) & (sib >= 0))
    def _():
        run([(0, own, *load(own, q0, g0), st0[own]), (1, sib, *load(sib, q1, g1), st1[sib])])

    @pl.when((own >= 0) != (sib >= 0))
    def _():
        block = jnp.maximum(own, sib)
        side = jnp.where(own >= 0, 0, 1)

        @pl.when(side == 0)
        def _():
            q_buf[...], g_buf[...] = load(block, q0, g0)

        @pl.when(side == 1)
        def _():
            q_buf[...], g_buf[...] = load(block, q1, g1)

        stats = jnp.where(side == 0, st0[block], st1[block])
        run([(side, block, q_buf[...], g_buf[...], stats)])

    @pl.when((own < 0) & (sib < 0))
    def _():
        buf[...] = jnp.zeros_like(buf)

    for i, out_ref in enumerate(outs):

        @pl.when((at >= out_offsets[i]) & (at < out_offsets[i + 1]))
        def _():
            out_ref[0] = buf[...]

    @pl.when(at == pl.num_programs(0) - 1)
    def _():
        out0[...] = dq[0].astype(out0.dtype)
        out1[...] = dq[1].astype(out1.dtype)


def remote_grads(table, own, sib, stats, groups, bases, out_sizes, carried, scale2):
    heads, _, width = own.shape
    rows = stats[0].shape[0] * QB
    count = len(bases)
    once = pl.Buffered(1)
    q_spec = pl.BlockSpec((heads, rows, width), lambda k, t: (0, 0, 0), pipeline_mode=once)
    g_spec = pl.BlockSpec((heads, rows, width), lambda k, t: (0, 1, 0), pipeline_mode=once)
    stat = pl.BlockSpec(stats[0].shape, lambda k, t: (0, 0, 0))
    acc_spec = pl.BlockSpec((heads, rows, width), lambda k, t: (0, 0, 0))

    def piece(start, size):
        return pl.BlockSpec(
            (1, 2, rows, width), lambda k, t: (jnp.clip(k - start, 0, size - 1), 0, 0, 0)
        )

    operands = [array for group in groups for array in group]
    offsets = [0]
    for array in operands:
        offsets.append(offsets[-1] + array.shape[0])
    out_offsets = [0]
    for size in out_sizes:
        out_offsets.append(out_offsets[-1] + size)
    acc = jax.ShapeDtypeStruct((heads, rows, width), jnp.bfloat16)
    return pl.pallas_call(
        functools.partial(remote_kernel, scale2, bases, offsets, out_offsets, not carried),
        grid_spec=pltpu.PrefetchScalarGridSpec(
            num_scalar_prefetch=1,
            grid=(SIDE * count,),
            in_specs=[q_spec, g_spec, q_spec, g_spec, stat, stat]
            + [piece(start, array.shape[0]) for start, array in zip(offsets, operands)]
            + [q_spec] * len(carried),
            out_specs=[acc_spec, acc_spec]
            + [piece(start, size) for start, size in zip(out_offsets, out_sizes)],
            scratch_shapes=[
                pltpu.VMEM((2, rows, width), jnp.bfloat16),
                pltpu.VMEM((heads * QB, width), jnp.bfloat16),
                pltpu.VMEM((heads * QB, width), jnp.bfloat16),
                pltpu.VMEM((2, heads, rows, width), jnp.float32),
            ],
        ),
        out_shape=[acc, acc]
        + [jax.ShapeDtypeStruct((size, 2, rows, width), jnp.bfloat16) for size in out_sizes],
        compiler_params=pltpu.CompilerParams(vmem_limit_bytes=VMEM_LIMIT),
        cost_estimate=pl.CostEstimate(
            flops=SIDE * count * 10 * heads * QB * rows * width,
            bytes_accessed=(8 + 4 * count) << 20,
            transcendentals=0,
        ),
        name="remote",
    )(table, own, own, sib, sib, *stats, *operands, *carried)


def split3(value):
    terms = []
    for _ in range(3):
        term = lax.reduce_precision(value, 8, 7)
        terms.append(term.astype(jnp.bfloat16))
        value = value - term
    return jnp.stack(terms, axis=-2)


def grads(queries, key_rows, value_rows, out_grad, outputs, logsumexp, selections):
    rows, kv_heads, _, width = queries.shape
    blocks = rows // QB
    scale = width ** (-0.5)
    scale2 = scale * LOG2E
    me = lax.axis_index("ctx")
    head = lax.axis_index("head")
    x, z, core = me // (2 * SIDE), (me // 2) % SIDE, me % 2

    keys = lax.dynamic_index_in_dim(key_rows, head, 1, keepdims=False)
    values = lax.dynamic_index_in_dim(value_rows, head, 1, keepdims=False)
    both = jnp.stack([keys, values])
    behind = shift(both, 0, 1)
    ahead = shift(both, 0, -1)
    across = shift(both, 0, 2)
    sides = jnp.stack([behind, ahead])
    line = (both[None], sides, across[None])
    line_behind = tuple(shift(piece, 1, 1) for piece in line)
    line_ahead = tuple(shift(piece, 1, -1) for piece in line)
    line_across = (
        shift(line_behind[0], 1, 1), shift(line_ahead[1], 1, -1), shift(line_behind[2], 1, 1)
    )

    def turn(value):
        return lax.all_to_all(value, "head", split_axis=0, concat_axis=0, tiled=True)

    delta = jnp.sum(out_grad.astype(jnp.float32) * outputs.astype(jnp.float32), axis=-1)
    stats = jnp.stack([logsumexp[:, 0] * LOG2E, delta[:, :, 0].T], axis=1)
    stats = split3(stats.reshape(kv_heads, 2, rows)).reshape(kv_heads, -1, width)
    own = turn(
        jnp.concatenate(
            [
                jnp.transpose(queries[:, :, 0], (1, 0, 2)),
                jnp.transpose(out_grad[:, :, 0], (1, 0, 2)),
                stats,
            ],
            axis=1,
        ),
    )
    sib = other_core(own)
    sib_selections = other_core(selections)

    def stats_of(packed):
        terms = packed[:, 2 * rows :].reshape(-1, 2, 3, blocks, QB).astype(jnp.float32)
        return (terms[:, :, 0] + terms[:, :, 1] + terms[:, :, 2]).transpose(2, 1, 0, 3).reshape(blocks, 2, -1)

    own_stats, sib_stats = stats_of(own), stats_of(sib)

    index = jnp.arange(SIDE * SIDE, dtype=jnp.int32)
    near, far = index % SIDE, index // SIDE
    near = jnp.where(near >= 2, 5 - near, near)
    back_x, back_z = jnp.where(core == 0, near, far), jnp.where(core == 0, far, near)
    source = (((x - back_x) % SIDE) * SIDE + (z - back_z) % SIDE) * 2 + core

    def listed(picks, device):
        hit = ((picks[:, 1:2] == source) | (picks[:, 2:3] == source)) & (source != device)
        return jnp.max(jnp.where(hit, jnp.arange(blocks, dtype=jnp.int32)[:, None], -1), axis=0)

    table = jnp.concatenate(
        [listed(selections, me), listed(sib_selections, me + 1 - 2 * core)]
    )

    def remote(groups, bases, out_sizes, carried=()):
        return remote_grads(
            table, own, sib, (own_stats, sib_stats), groups, bases, out_sizes, carried, scale2
        )

    first0, first1, part_behind, part_ahead = remote(
        [line_behind, line_ahead], (SIDE, 3 * SIDE), (SIDE, SIDE)
    )
    back_behind = shift(part_behind, 1, -1)
    back_ahead = shift(part_ahead, 1, 1)
    second0, second1, *part_across, part_line = remote(
        [line_across, line], (2 * SIDE, 0), (1,) * SIDE + (SIDE,), (first0, first1)
    )
    part_across = [part[0] for part in part_across]
    own_q, own_k, own_v = own_grads(own, own_stats, keys, values, scale2)

    def summed(*parts):
        return sum(part.astype(jnp.float32) for part in parts)

    def spread(parts):
        return (shift(parts[0], 0, -1), shift(parts[1], 0, 1), shift(parts[2], 0, 2))

    side = spread(part_across[1:])
    far_sum = summed(part_across[0], *side).astype(jnp.bfloat16)
    total = [summed(part_line[i], back_behind[i], back_ahead[i]) for i in range(SIDE)]
    low = [part.astype(jnp.bfloat16) for part in total[1:]]
    received = spread(low)
    received += (shift(far_sum, 1, 2),)

    def final(i, own_part, factor):
        return ((total[0][i] + summed(*(part[i] for part in received)) + own_part) * factor).astype(
            jnp.bfloat16
        )

    grad_k, grad_v = final(0, own_k, scale), final(1, own_v, 1.0)

    returned = other_core(second1)
    dq = ((own_q + summed(second0, returned)) * scale).astype(jnp.bfloat16)
    dq = jnp.transpose(turn(dq), (1, 0, 2))[:, :, None]
    return dq, grad_k[:, None], grad_v[:, None]


def solution(mesh):
    in_specs = (
        P("ctx", None, "head", None),
        P("ctx", None, None),
        P("ctx", None, None),
        P("ctx", None, "head", None),
        P("ctx", None, "head", None),
        P(None, "head", "ctx"),
        P("ctx", None),
    )
    out_specs = (P("ctx", None, "head", None), P("ctx", "head", None), P("ctx", "head", None))
    return jax.shard_map(grads, mesh=mesh, in_specs=in_specs, out_specs=out_specs, check_vma=False)
```
